32 devices in a mesh: groups: 2 (over x), seqt: 16 (over z, y, core).
Axes of the slice: x: 2, y: 2, z: 4, core: 2. Of those that a mesh axis runs over, the one named last changes fastest.
Arguments:
- out_grad: bfloat16 [4096, 4096], P(('groups', 'seqt')), parts along dimension 0, may hold values from -6 to 6
- hidden: bfloat16 [4096, 16384], P(('groups', 'seqt')), parts along dimension 0, may hold values from -0.13183594 to 0.13183594
- down_tiles: bfloat16 [128, 4, 128, 128], P('seqt'), may hold values from -0.3125 to 0.3125
- row_blocks: int32 [16, 4], replicated, may hold values from 0 to 31, as said below
- tile_mask: int32 [128, 4], P('seqt'), may hold values 0 or 1
Outputs:
- grad_hidden: bfloat16 [4096, 16384], P(('groups', 'seqt')), parts along dimension 0
- grad_tiles: float32 [256, 4, 128, 128], P(('groups', 'seqt')), parts along dimension 0
The draws below stay inside these ranges and needn't reach their ends.
There are 2 independent parts, one for each index of `groups`. The reference program is written for one: setup_inputs(seed, part) draws one part's arguments, and reference() takes and returns one part's arrays. A program takes and returns all parts, laid end to end along the dimension named above; an argument that names none is the same for every part. Nothing has to cross between parts.
Inputs may be any that keep to these rules, and one draw needn't show every extreme that they name: `row_blocks`: the 4 row blocks of one device are distinct.
All inputs are finite; a program needn't handle non-finite values. No bound on the sum of `tile_mask` on one device may be relied on, other than what follows from the above.
Results may differ from the reference program's by a relative error of at most 0.001.
Values may be sent and summed in bfloat16 or wider, within the bound.
No kernel may reach another device: no remote copies, remote signals or barrier semaphores. Data moves between devices by JAX's collectives and lax.ppermute only.
A program may use at most 128 MiB of HBM per device.

```python
import jax
import jax.numpy as jnp
from jax import lax

D = 4096
FF = 16384
TILE = 128
RSET = 4
TOK_DEV = 128
TOKENS = 2048
RT = 32
CT = 128
N_SEQT = 16


def draw_row_blocks(key, part):
    subkeys = jax.random.split(key, N_SEQT)

    def device_rows(subkey):
        return jax.random.permutation(subkey, RT)[:RSET]
    return jax.vmap(device_rows)(subkeys).astype(jnp.int32)


def with_ends(values, stream_key, low, top_value):
    dims = values.shape
    spot = [jax.random.randint(jax.random.fold_in(stream_key, axis), (), 0, dims[axis]) for axis in range(len(dims))]
    values = values.at[tuple(spot)].set(low)
    longest = dims.index(max(dims))
    spot[longest] = (spot[longest] + 1) % dims[longest]
    return values.at[tuple(spot)].set(top_value)


def block_scale(rng, dims, cuts, smallest, largest):
    factor_of, own = 1.0, jax.random.fold_in(rng, 6)
    for position, parts in cuts:
        steps = jnp.exp(jax.random.uniform(jax.random.fold_in(own, position), (parts,), jnp.float32, smallest / len(cuts), largest / len(cuts)))
        factor_of = factor_of * jnp.repeat(steps, dims[position] // parts).reshape([-1 if axis == position else 1 for axis in range(len(dims))])
    return factor_of


def noise(key, shape, width, limit, pieces=(), kind=jnp.bfloat16):
    values = jax.random.normal(key, shape, jnp.float32) * width
    if len(pieces) > 0:
        values = block_scale(key, shape, pieces, -0.22, 0.18) * values
    return jnp.clip(values, min=-limit, max=limit).astype(kind)


def setup_inputs(seed: int = 0, part: int = 0) -> dict:
    arg_keys = jax.random.split(jax.random.key(seed), 6)
    own_keys = jax.random.split(jax.random.fold_in(arg_keys[5], part), 6)
    return {
        "out_grad": noise(own_keys[0], (TOKENS, D), 1.0, 6.0, ((0, 16),)),
        "hidden": noise(own_keys[1], (TOKENS, FF), ((TOK_DEV * N_SEQT) ** -0.5), 0.13183594, ((0, 16),)),
        "down_tiles": noise(arg_keys[2], (CT, RSET, TILE, TILE), (RSET * TILE * 4 // 5) ** -0.5, 0.3125, ((0, 16),)),
        "row_blocks": draw_row_blocks(jax.random.fold_in(arg_keys[5], 71), part),
        "tile_mask": with_ends((jax.random.randint(arg_keys[4], (CT, RSET), 0, 5) < 4).astype(jnp.int32), jax.random.fold_in(arg_keys[4], 1), 0, 1),
    }


def reference(out_grad, hidden, down_tiles, row_blocks, tile_mask):
    token_count = out_grad.shape[0]
    col_count = FF // (TILE * N_SEQT)
    grad_blocks = out_grad.reshape(token_count, D // TILE, TILE)
    tiles_dev = down_tiles.reshape(N_SEQT, col_count, RSET, TILE, TILE)
    masks_dev = tile_mask.reshape(N_SEQT, col_count, RSET)

    def per_device(device):
        row_list = lax.dynamic_index_in_dim(row_blocks, device, 0, keepdims=False)
        picked = jnp.take(grad_blocks, row_list, axis=1).reshape(token_count, RSET * TILE)
        tile_set = lax.dynamic_index_in_dim(tiles_dev, device, 0, keepdims=False)
        mask_set = lax.dynamic_index_in_dim(masks_dev, device, 0, keepdims=False)
        masked = tile_set * mask_set[:, :, None, None].astype(tile_set.dtype)
        weight_mat = masked.transpose(0, 2, 1, 3).reshape(col_count * TILE, RSET * TILE)
        grad_local = jnp.dot(picked, weight_mat.T, preferred_element_type=jnp.float32).astype(jnp.bfloat16)
        start_col = (device * (col_count * TILE)).astype(jnp.int32)
        columns = lax.dynamic_slice_in_dim(hidden, start_col, col_count * TILE, 1)
        products = jnp.dot(columns.T, picked, preferred_element_type=jnp.float32)
        tile_grads = products.reshape(col_count, TILE, RSET, TILE).transpose(0, 2, 1, 3)
        tile_grads = tile_grads * mask_set[:, :, None, None].astype(jnp.float32)
        return grad_local, tile_grads

    grad_parts, tile_parts = lax.map(per_device, jnp.arange(N_SEQT, dtype=jnp.int32))
    grad_hidden = grad_parts.transpose(1, 0, 2).reshape(token_count, FF)
    grad_tiles = tile_parts.reshape(FF // TILE, RSET, TILE, TILE)
    return grad_hidden, grad_tiles
```

```python
import functools

import jax
import jax.numpy as jnp
from jax import lax
from jax.experimental import pallas as pl
from jax.experimental.pallas import tpu as pltpu
from jax.sharding import PartitionSpec as P


PLANES = 4
TOP = 32000.0
ANY = pl.BlockSpec(memory_space=pl.ANY)
SMEM = pl.BlockSpec(memory_space=pltpu.SMEM)
VMEM = pl.BlockSpec(memory_space=pltpu.VMEM)


def run_copies(copies, sems):
    started = []
    for n, (src, dst) in enumerate(copies):
        copy = pltpu.make_async_copy(src, dst, sems.at[n])
        copy.start()
        started.append(copy)
    return started


def wait_all(started):
    for copy in started:
        copy.wait()


def pack_kernel(width, count, idx_ref, hidden_ref, *refs):
    outs, sems = refs[:count], refs[count]
    wait_all(run_copies(
        [(hidden_ref.at[:, pl.ds(pl.multiple_of(idx_ref[n] * width, 128), width)], outs[n]) for n in range(count)],
        sems,
    ))


def unpack_kernel(width, count, aliased, idx_ref, *refs):
    ins = refs[:count]
    out, sems = refs[count + aliased], refs[count + aliased + 1]
    wait_all(run_copies(
        [(ins[n], out.at[:, pl.ds(pl.multiple_of(idx_ref[n] * width, 128), width)]) for n in range(count)],
        sems,
    ))


def pick_copies(rows_ref, og_refs, picks, tokens, tile, slots):
    return [
        (og.at[:, pl.ds(pl.multiple_of(rows_ref[k] * tile, 128), tile)],
         picks.at[pl.ds(p * tokens, tokens), pl.ds(k * tile, tile)])
        for p, og in enumerate(og_refs) for k in range(slots)
    ]


def decode(ref, tiles, tile, n):
    scale = jnp.exp2(ref[pl.ds(tiles * tile + n, 1), :].astype(jnp.float32)) * (1.0 / TOP)
    start = n * tile
    if not isinstance(n, int):
        start = pl.multiple_of(start, tile)
    return ref[pl.ds(start, tile), :].astype(jnp.float32) * scale


def partial_kernel(dims, adds, coded, rows_ref, pos_ref, *refs):
    members, tokens, cols, slots, tile = dims
    og_refs, refs = refs[:members], refs[members:]
    hidden_ref, refs = refs[0], refs[1:]
    h_refs, refs = refs[:members - 1], refs[members - 1:]
    add_refs, refs = refs[:adds], refs[adds:]
    out, picks, held, total, sems = refs
    width = cols * tile
    copies = pick_copies(rows_ref, og_refs, picks, tokens, tile, slots)
    copies.append((hidden_ref.at[:, pl.ds(pl.multiple_of(pos_ref[0] * width, 128), width)], held.at[pl.ds(0, tokens), :]))
    copies += [(h, held.at[pl.ds((p + 1) * tokens, tokens), :]) for p, h in enumerate(h_refs)]
    wait_all(run_copies(copies, sems))
    total[...] = lax.dot_general(held[...], picks[...], (((0,), (0,)), ((), ())), preferred_element_type=jnp.float32)
    tiles = cols * slots
    for n in range(tiles):
        c, k = divmod(n, slots)
        value = total[pl.ds(c * tile, tile), pl.ds(k * tile, tile)]
        for add in add_refs:
            value = value + decode(add, tiles, tile, n)
        if coded:
            top = jnp.max(jnp.abs(value), axis=0, keepdims=True)
            power = jnp.ceil(jnp.log2(jnp.maximum(top, 1e-30)))
            code = jnp.round(value * (jnp.exp2(-power) * TOP))
            out[pl.ds(n * tile, tile), :] = code.astype(jnp.int32).astype(jnp.int16)
            total[pl.ds(n, 1), pl.ds(0, tile)] = power
        else:
            out[pl.ds(n * tile, tile), :] = value


def finish_kernel(dims, adds, mask_ref, own_ref, *refs):
    members, tokens, cols, slots, tile = dims
    add_refs, out = refs[:adds], refs[adds]
    tiles = cols * slots
    for n in range(tiles):
        c, k = divmod(n, slots)
        value = own_ref[pl.ds(n * tile, tile), :]
        for add in add_refs:
            value = value + decode(add, tiles, tile, n)
        out[c, k] = value * mask_ref[c, k].astype(jnp.float32)


def grad_kernel(dims, choices, rows_ref, pos_ref, *refs):
    members, tokens, cols, slots, tile = dims
    og_refs, refs = refs[:members], refs[members:]
    w_refs, refs = refs[:choices], refs[choices:]
    outs, refs = refs[:members], refs[members:]
    picks, weights, sems = refs
    copies = pick_copies(rows_ref, og_refs, picks, tokens, tile, slots)
    first = len(copies)
    started = run_copies(copies, sems)
    for n, w in enumerate(w_refs):
        @pl.when(pos_ref[1] == n)
        def _():
            wait_all(run_copies([(w.at[:, k], weights.at[:, :, pl.ds(k * tile, tile)]) for k in range(slots)], sems.at[pl.ds(first, slots)]))
    wait_all(started)
    matrix = weights[...].reshape(cols * tile, slots * tile)
    for p in range(members):
        rows = picks[pl.ds(p * tokens, tokens), :]
        outs[p][...] = lax.dot_general(rows, matrix, (((1,), (1,)), ((), ())), preferred_element_type=jnp.float32).astype(jnp.bfloat16)


def on_device(out_grad, hidden, down_tiles, row_blocks, tile_mask):
    devices = lax.axis_size("seqt")
    members = devices // PLANES
    tokens = out_grad.shape[0]
    cols, slots, tile = down_tiles.shape[:3]
    width = cols * tile
    tiles = cols * slots
    dims = (members, tokens, cols, slots, tile)
    scale_rows = -(-tiles // 16) * 16
    me = lax.axis_index("seqt")
    z, m = me // members, me % members
    even = z % 2 == 0
    low = z < 2
    outer = (z == 0) | (z == 3)
    plane = [jnp.where(even, 3, 0), z ^ 2, jnp.where(even, 1, 2), z]
    rows = [lax.dynamic_index_in_dim(row_blocks, q * members + m, 0, keepdims=False) for q in plane]

    def inside(value, p):
        return lax.ppermute(value, "seqt", [(i, i ^ p) for i in range(devices)])

    def across(value, pairs):
        return lax.ppermute(value, "seqt", [(a * members + i, b * members + i) for a, b in pairs for i in range(members)])

    og = {0: out_grad}
    bit = members // 2
    while bit:
        for p in list(og):
            with jax.named_scope(f"og_{p ^ bit}"):
                og[p ^ bit] = inside(og[p], bit)
        bit //= 2
    og = [og[p] for p in range(members)]

    with jax.named_scope("mask_weights"):
        masked = down_tiles * tile_mask[:, :, None, None].astype(down_tiles.dtype)
    up, down = [(0, 1), (1, 2), (2, 3)], [(3, 2), (2, 1), (1, 0)]
    w1p, w1m = across(masked, up), across(masked, down)
    w2p, w2m = across(w1p, up[1:]), across(w1m, down[1:])
    w2 = jnp.where(low, w2m, w2p)
    w3 = across(w2, [(2, 3), (1, 0)])

    parts = [(j, p) for j in range(PLANES) for p in range(1, members)]
    idx = jnp.stack([plane[j] * members + (m ^ p) for j, p in parts]).astype(jnp.int32)
    packed = pl.pallas_call(
        functools.partial(pack_kernel, width, len(parts)),
        out_shape=[jax.ShapeDtypeStruct((tokens, width), hidden.dtype)] * len(parts),
        in_specs=[SMEM, ANY],
        out_specs=[ANY] * len(parts),
        scratch_shapes=[pltpu.SemaphoreType.DMA((len(parts),))],
        name="pack",
    )(idx, hidden)
    h = [[None] * (members - 1) for _ in range(PLANES)]
    order = [2, 3, 1] if members == 4 else list(range(members - 1, 0, -1))
    for j in range(PLANES):
        for p in order:
            with jax.named_scope(f"h_{j}_{p}"):
                h[j][p - 1] = inside(packed[parts.index((j, p))], p)

    def position(j, choice=0):
        return jnp.stack([plane[j] * members + m, jnp.asarray(choice, jnp.int32)]).astype(jnp.int32)

    coded_shape = jax.ShapeDtypeStruct((tiles * tile + scale_rows, tile), jnp.int16)
    plain_shape = jax.ShapeDtypeStruct((tiles * tile, tile), jnp.float32)

    def partial(j, adds, coded=True):
        return pl.pallas_call(
            functools.partial(partial_kernel if not coded else coded_kernel, dims, len(adds), coded),
            out_shape=coded_shape if coded else plain_shape,
            in_specs=[SMEM, SMEM] + [ANY] * (2 * members) + [VMEM] * len(adds),
            out_specs=VMEM,
            scratch_shapes=[
                pltpu.VMEM((members * tokens, slots * tile), jnp.bfloat16),
                pltpu.VMEM((members * tokens, width), jnp.bfloat16),
                pltpu.VMEM((width, slots * tile), jnp.float32),
                pltpu.SemaphoreType.DMA((members * (slots + 1),)),
            ],
            name=f"partial_{j}_{len(adds)}",
        )(rows[j], position(j), *og, hidden, *h[j], *adds)

    def grads(j, weights, choice):
        return pl.pallas_call(
            functools.partial(grad_kernel, dims, len(weights)),
            out_shape=[jax.ShapeDtypeStruct((tokens, width), jnp.bfloat16)] * members,
            in_specs=[SMEM, SMEM] + [ANY] * (members + len(weights)),
            out_specs=[VMEM] * members,
            scratch_shapes=[
                pltpu.VMEM((members * tokens, slots * tile), jnp.bfloat16),
                pltpu.VMEM((cols, tile, slots * tile), jnp.bfloat16),
                pltpu.SemaphoreType.DMA(((members + 1) * slots,)),
            ],
            name=f"grad_{j}",
        )(rows[j], position(j, choice), *og, *weights)

    inward = [(0, 1), (3, 2)]
    outward = [(1, 0), (2, 3)]
    rise, fall = [(0, 1), (1, 2)], [(3, 2), (2, 1)]

    g = [None] * PLANES
    back = [None] * PLANES

    def give_back(j, weights, choice):
        g[j] = grads(j, weights, choice)
        back[j] = [g[j][0]]
        for p in range(1, members):
            with jax.named_scope(f"g_{j}_{p}"):
                back[j].append(inside(g[j][p], p))

    give_back(3, [masked], 0)
    s1 = partial(0, [])
    r1 = across(s1, inward)
    s2 = partial(1, [r1])
    r2p, r2m = across(s2, rise), across(s2, fall)
    give_back(2, [w1m, w1p], jnp.where(low, 0, 1))
    near = jnp.where(low, r2p, r2m)
    far = jnp.where(low, r2m, r2p)
    s3 = partial(2, [near])
    r3p, r3m = across(s3, rise), across(s3, fall)
    s4 = partial(0, [far])
    r4 = across(s4, outward)
    give_back(1, [w2], 0)
    give_back(0, [w3, w1p, w1m], jnp.where(outer, 0, jnp.where(low, 1, 2)))
    own = partial(3, [], coded=False)
    grad_tiles = pl.pallas_call(
        functools.partial(finish_kernel, dims, 3),
        out_shape=jax.ShapeDtypeStruct((cols, slots, tile, tile), jnp.float32),
        in_specs=[SMEM] + [VMEM] * 4,
        out_specs=VMEM,
        name="finish",
    )(tile_mask, own, r3p, r3m, r4)

    result = None
    for j in (3, 2, 1, 0):
        places = jnp.stack([plane[j] * members + (m ^ p) for p in range(members)]).astype(jnp.int32)
        extra = [] if result is None else [result]
        result = pl.pallas_call(
            functools.partial(unpack_kernel, width, members, len(extra)),
            out_shape=jax.ShapeDtypeStruct(hidden.shape, jnp.bfloat16),
            in_specs=[SMEM] + [ANY] * (members + len(extra)),
            out_specs=ANY,
            scratch_shapes=[pltpu.SemaphoreType.DMA((members,))],
            input_output_aliases={1 + members: 0} if extra else {},
            name=f"unpack_{j}",
        )(places, *back[j], *extra)
    return result, grad_tiles


def coded_kernel(dims, adds, coded, rows_ref, pos_ref, *refs):
    partial_kernel(dims, adds, coded, rows_ref, pos_ref, *refs)
    cols, slots, tile = dims[2:]
    out, total = refs[-5], refs[-2]
    tiles = cols * slots
    scale_rows = out.shape[0] - tiles * tile
    powers = total[pl.ds(0, scale_rows), pl.ds(0, tile)]
    out[pl.ds(tiles * tile, scale_rows), :] = powers.astype(jnp.int32).astype(jnp.int16)


def solution(mesh):
    return jax.shard_map(
        on_device,
        mesh=mesh,
        in_specs=(
            P(("groups", "seqt"), None),
            P(("groups", "seqt"), None),
            P("seqt", None, None, None),
            P(),
            P("seqt", None),
        ),
        out_specs=(P(("groups", "seqt"), None), P(("groups", "seqt"), None, None, None)),
        check_vma=False,
    )
```

```python
import functools

import jax
import jax.numpy as jnp
from jax import lax
from jax.experimental import pallas as pl
from jax.experimental.pallas import tpu as pltpu
from jax.sharding import PartitionSpec as P


PLANES = 4
TOP = 32000.0
LIMIT = 64 * 1024 * 1024
HBM = pl.BlockSpec(memory_space=pltpu.HBM)
SMEM = pl.BlockSpec(memory_space=pltpu.SMEM)
VMEM = pl.BlockSpec(memory_space=pltpu.VMEM)
DMA = pltpu.SemaphoreType.DMA


def start_all(copies, sems):
    started = []
    for n, (src, dst) in enumerate(copies):
        copy = pltpu.make_async_copy(src, dst, sems.at[n])
        copy.start()
        started.append(copy)
    return started


def wait_all(started):
    for copy in started:
        copy.wait()


def plane_of(j, z):
    even = z % 2 == 0
    if j == 0:
        return jnp.where(even, 3, 0)
    if j == 1:
        return jnp.where(z < 2, z + 2, z - 2)
    if j == 2:
        return jnp.where(even, 1, 2)
    return z


def owner(j, p, members, me_ref):
    z, m = me_ref[0] // members, me_ref[0] % members
    return plane_of(j, z) * members + (m ^ p)


def block(index, size):
    return pl.ds(pl.multiple_of(index * size, 128), size)


def own_copies(dims, who, rows_ref, grad_ref, hidden_ref, picks, held):
    _, _, cols, slots, tile = dims
    width = cols * tile
    copies = []
    if held is not None:
        copies.append((hidden_ref.at[:, block(who, width)], held))
    for k in range(slots):
        copies.append((grad_ref.at[:, block(rows_ref[k, who], tile)], picks.at[:, pl.ds(k * tile, tile)]))
    return copies


def pack_kernel(dims, chunks, me_ref, rows_ref, grad_ref, hidden_ref, *refs):
    members, _, cols, slots, tile = dims
    outs, sems = refs[:-1], refs[-1]
    width = cols * tile
    copies = []
    for n, j in enumerate(chunks):
        for p in range(1, members):
            out = outs[n * (members - 1) + p - 1]
            copies += own_copies(dims, owner(j, p, members, me_ref), rows_ref, grad_ref, hidden_ref,
                                 out.at[:, pl.ds(width, slots * tile)], out.at[:, pl.ds(0, width)])
    wait_all(start_all(copies, sems))


def mask_kernel(cols, slots, mask_ref, tiles_ref, out):
    for c in range(cols):
        for k in range(slots):
            out[c, k] = tiles_ref[c, k] * mask_ref[k, c].astype(jnp.float32).astype(jnp.bfloat16)


def decode(ref, tiles, tile, n):
    scale = jnp.exp2(ref[pl.ds(tiles * tile + n, 1), :].astype(jnp.float32)) * (1.0 / TOP)
    return ref[pl.ds(n * tile, tile), :].astype(jnp.float32) * scale


def encode(value, out, powers, tile, n):
    top = jnp.max(jnp.abs(value), axis=0, keepdims=True)
    power = jnp.ceil(jnp.log2(jnp.maximum(top, 1e-30)))
    code = jnp.round(value * (jnp.exp2(-power) * TOP))
    out[pl.ds(n * tile, tile), :] = code.astype(jnp.int32).astype(jnp.int16)
    powers[pl.ds(n, 1), :] = power


def flush_powers(out, powers, first):
    rows = out.shape[0] - first
    out[pl.ds(first, rows), :] = powers[...].astype(jnp.int32).astype(jnp.int16)


def matmul_tiles(dims, j, me_ref, rows_ref, grad_ref, hidden_ref, parts, extra, picks, held, total, sems):
    members, tokens, cols, slots, tile = dims
    width = cols * tile
    first = pl.ds(0, tokens)
    copies = own_copies(dims, owner(j, 0, members, me_ref), rows_ref, grad_ref, hidden_ref, picks.at[first, :], held.at[first, :])
    for p, part in enumerate(parts):
        rows = pl.ds((p + 1) * tokens, tokens)
        copies.append((part.at[:, pl.ds(0, width)], held.at[rows, :]))
        copies.append((part.at[:, pl.ds(width, slots * tile)], picks.at[rows, :]))
    started = start_all(copies + extra, sems)
    wait_all(started[:len(copies)])
    total[...] = lax.dot_general(held[...], picks[...], (((0,), (0,)), ((), ())), preferred_element_type=jnp.float32)
    return started[len(copies):]


def partial_kernel(dims, j, coded, me_ref, rows_ref, grad_ref, hidden_ref, *refs):
    members, _, cols, slots, tile = dims
    tiles = cols * slots
    parts, (out, picks, held, total, sems, *powers) = refs[:members - 1], refs[members - 1:]
    matmul_tiles(dims, j, me_ref, rows_ref, grad_ref, hidden_ref, parts, [], picks, held, total, sems)
    for n in range(tiles):
        c, k = divmod(n, slots)
        value = total[pl.ds(c * tile, tile), pl.ds(k * tile, tile)]
        if coded:
            encode(value, out, powers[0], tile, n)
        else:
            out[pl.ds(n * tile, tile), :] = value
    if coded:
        flush_powers(out, powers[0], tiles * tile)


def join_kernel(dims, base, added, out, powers):
    _, _, cols, slots, tile = dims
    tiles = cols * slots
    for n in range(tiles):
        encode(base[pl.ds(n * tile, tile), :] + decode(added, tiles, tile, n), out, powers, tile, n)
    flush_powers(out, powers, tiles * tile)


def third_kernel(dims, j, me_ref, rows_ref, grad_ref, hidden_ref, *refs):
    members, _, cols, slots, tile = dims
    tiles = cols * slots
    parts, (first, rose, fell, near_out, far_out, picks, held, total, sems, powers, base, arrived) = refs[:members - 1], refs[members - 1:]
    extra = [(rose, arrived.at[0]), (fell, arrived.at[1]), (first, base)]
    pending = matmul_tiles(dims, j, me_ref, rows_ref, grad_ref, hidden_ref, parts, extra, picks, held, total, sems)
    wait_all(pending)
    near = jnp.where(me_ref[0] < 2 * members, 0, 1)
    for n in range(tiles):
        c, k = divmod(n, slots)
        value = total[pl.ds(c * tile, tile), pl.ds(k * tile, tile)] + decode(arrived.at[near], tiles, tile, n)
        encode(value, near_out, powers, tile, n)
    flush_powers(near_out, powers, tiles * tile)
    for n in range(tiles):
        value = decode(base, tiles, tile, n) + decode(arrived.at[1 - near], tiles, tile, n)
        encode(value, far_out, powers, tile, n)
    flush_powers(far_out, powers, tiles * tile)


def finish_kernel(dims, me_ref, mask_ref, own_ref, rose, fell, last, out, own, arrived, made, in_sems, out_sems):
    members, _, cols, slots, tile = dims
    tiles = cols * slots
    tail = pl.ds(tiles * tile, rose.shape[0] - tiles * tile)
    sources = (rose, fell, last)
    heads = start_all([(src.at[tail, :], arrived.at[n, tail, :]) for n, src in enumerate(sources)], in_sems.at[cols])
    chunks = []
    for c in range(cols):
        rows = pl.ds(c * slots * tile, slots * tile)
        copies = [(src.at[rows, :], arrived.at[n, rows, :]) for n, src in enumerate(sources)] + [(own_ref.at[rows, :], own.at[rows, :])]
        chunks.append(start_all(copies, in_sems.at[c]))
    outer = (me_ref[0] < members) | (me_ref[0] >= 3 * members)
    slot = jnp.where(outer, 2, 0)
    wait_all(heads)
    writes = []
    for c in range(cols):
        wait_all(chunks[c])
        for k in range(slots):
            n = c * slots + k
            value = own[pl.ds(n * tile, tile), :] + decode(arrived.at[slot], tiles, tile, n) + decode(arrived.at[1], tiles, tile, n)
            made[c, k] = value * mask_ref[k, c].astype(jnp.float32)
        write = pltpu.make_async_copy(made.at[c], out.at[c], out_sems.at[c])
        write.start()
        writes.append(write)
    wait_all(writes)


def grad_kernel(dims, j, choices, me_ref, rows_ref, grad_ref, *refs):
    members, tokens, cols, slots, tile = dims
    width = cols * tile
    parts, refs = refs[:members - 1], refs[members - 1:]
    w_refs, refs = refs[:choices], refs[choices:]
    outs, (picks, weights, sems) = refs[:members], refs[members:]
    copies = own_copies(dims, owner(j, 0, members, me_ref), rows_ref, grad_ref, None, picks.at[pl.ds(0, tokens), :], None)
    for p, part in enumerate(parts):
        copies.append((part.at[:, pl.ds(width, slots * tile)], picks.at[pl.ds((p + 1) * tokens, tokens), :]))
    high = jnp.where(me_ref[0] < 2 * members, 0, 1)
    outer = (me_ref[0] < members) | (me_ref[0] >= 3 * members)
    choice = high
    if choices == 4:
        choice = jnp.where(outer, 2 + high, high)
    if choices == 1:
        choice = 0 * high
    started = start_all(copies, sems)
    for n, w in enumerate(w_refs):
        @pl.when(choice == n)
        def _():
            wait_all(start_all([(w.at[:, k], weights.at[:, :, pl.ds(k * tile, tile)]) for k in range(slots)], sems.at[pl.ds(len(copies), slots)]))
    wait_all(started)
    matrix = weights[...].reshape(width, slots * tile)
    for p in range(members):
        rows = picks[pl.ds(p * tokens, tokens), :]
        outs[p][...] = lax.dot_general(rows, matrix, (((1,), (1,)), ((), ())), preferred_element_type=jnp.float32).astype(jnp.bfloat16)


def unpack_kernel(dims, chunks, aliased, me_ref, *refs):
    members, _, cols, _, tile = dims
    width = cols * tile
    count = len(chunks) * members
    ins, out, sems = refs[:count], refs[count + aliased], refs[-1]
    places = [owner(j, p, members, me_ref) for j in chunks for p in range(members)]
    wait_all(start_all([(ins[n], out.at[:, block(places[n], width)]) for n in range(count)], sems))


def on_device(out_grad, hidden, down_tiles, row_blocks, tile_mask):
    devices = lax.axis_size("seqt")
    members = devices // PLANES
    tokens = out_grad.shape[0]
    cols, slots, tile = down_tiles.shape[:3]
    width, tiles = cols * tile, cols * slots
    dims = (members, tokens, cols, slots, tile)
    scale_rows = -(-tiles // 16) * 16
    me = jnp.full((1,), lax.axis_index("seqt"), jnp.int32)
    row_blocks, tile_mask = row_blocks.T, tile_mask.T
    bf16, f32 = jnp.bfloat16, jnp.float32
    half = members // 2
    partners = sorted(range(1, members), key=lambda p: (p < half, p))

    def call(kernel, operands, specs, outs, out_specs, scratch, **extra):
        return pl.pallas_call(
            kernel, out_shape=outs, in_specs=specs, out_specs=out_specs,
            scratch_shapes=scratch, compiler_params=pltpu.CompilerParams(vmem_limit_bytes=LIMIT), **extra,
        )(*operands)

    def permute(value, pairs):
        return lax.ppermute(value, "seqt", pairs)

    def inside(value, p):
        return permute(value, [(i, i ^ p) for i in range(devices)])

    def across(value, pairs):
        return permute(value, [(a * members + i, b * members + i) for a, b in pairs for i in range(members)])

    parts = [None] * PLANES
    for chunks in ((0,), (1, 2, 3)):
        count = len(chunks) * (members - 1)
        packed = call(
            functools.partial(pack_kernel, dims, chunks),
            (me, row_blocks, out_grad, hidden), [SMEM, SMEM, HBM, HBM],
            [jax.ShapeDtypeStruct((tokens, width + slots * tile), bf16)] * count,
            [VMEM] * count, [DMA((count * (slots + 1),))],
        )
        for n, j in enumerate(chunks):
            parts[j] = [None] * (members - 1)
            for p in partners:
                parts[j][p - 1] = inside(packed[n * (members - 1) + p - 1], p)

    masked = call(
        functools.partial(mask_kernel, cols, slots), (tile_mask, down_tiles), [SMEM, VMEM],
        jax.ShapeDtypeStruct(down_tiles.shape, bf16), VMEM, [],
    )
    up, down = [(0, 1), (1, 2), (2, 3)], [(3, 2), (2, 1), (1, 0)]
    w1p, w1m = across(masked, up), across(masked, down)
    w2p, w2m = across(w1p, up[1:]), across(w1m, down[1:])
    w3p, w3m = across(w2p, up[2:]), across(w2m, down[2:])

    coded_shape = jax.ShapeDtypeStruct((tiles * tile + scale_rows, tile), jnp.int16)
    plain_shape = jax.ShapeDtypeStruct((tiles * tile, tile), f32)
    powers = pltpu.VMEM((scale_rows, tile), f32)
    matmul_scratch = [
        pltpu.VMEM((members * tokens, slots * tile), bf16),
        pltpu.VMEM((members * tokens, width), bf16),
        pltpu.VMEM((width, slots * tile), f32),
        DMA((2 * members + slots + 4,)),
    ]

    def partial(j, coded):
        return call(
            functools.partial(partial_kernel, dims, j, coded),
            (me, row_blocks, out_grad, hidden, *parts[j]), [SMEM, SMEM] + [HBM] * (members + 1),
            coded_shape if coded else plain_shape, VMEM, matmul_scratch + [powers] * coded,
        )

    back = [None] * PLANES

    def give_back(j, weights):
        products = call(
            functools.partial(grad_kernel, dims, j, len(weights)),
            (me, row_blocks, out_grad, *parts[j], *weights), [SMEM, SMEM] + [HBM] * (members + len(weights)),
            [jax.ShapeDtypeStruct((tokens, width), bf16)] * members, [VMEM] * members,
            [
                pltpu.VMEM((members * tokens, slots * tile), bf16),
                pltpu.VMEM((cols, tile, slots * tile), bf16),
                DMA((members + 2 * slots,)),
            ],
        )
        arrived = {p: inside(products[p], p) for p in partners}
        back[j] = [products[0]] + [arrived[p] for p in range(1, members)]

    rise, fall = [(0, 1), (1, 2)], [(3, 2), (2, 1)]
    s1 = partial(0, True)
    r1 = across(s1, [(0, 1), (3, 2)])
    s2 = call(functools.partial(join_kernel, dims), (partial(1, False), r1), [VMEM, VMEM], coded_shape, VMEM, [powers])
    r2p, r2m = across(s2, rise), across(s2, fall)
    coded_buffer = pltpu.VMEM(coded_shape.shape, jnp.int16)
    s3, s4 = call(
        functools.partial(third_kernel, dims, 2),
        (me, row_blocks, out_grad, hidden, *parts[2], s1, r2p, r2m), [SMEM, SMEM] + [HBM] * (members + 4),
        [coded_shape, coded_shape], [VMEM, VMEM],
        matmul_scratch + [powers, coded_buffer, pltpu.VMEM((2, *coded_shape.shape), jnp.int16)],
    )
    r3p, r3m = across(s3, rise), across(s3, fall)
    r4 = across(s4, [(1, 0), (2, 3)])
    own = partial(3, False)

    give_back(1, [w2m, w2p])
    give_back(2, [w1m, w1p])
    give_back(3, [masked])
    give_back(0, [w1p, w1m, w3m, w3p])

    grad_tiles = call(
        functools.partial(finish_kernel, dims), (me, tile_mask, own, r3p, r3m, r4),
        [SMEM, SMEM] + [HBM] * 4, jax.ShapeDtypeStruct((cols, slots, tile, tile), f32), HBM,
        [
            pltpu.VMEM(plain_shape.shape, f32),
            pltpu.VMEM((3, *coded_shape.shape), jnp.int16),
            pltpu.VMEM((cols, slots, tile, tile), f32),
            DMA((cols + 1, 4)), DMA((cols,)),
        ],
    )

    def unpack(chunks, extra):
        pieces = [piece for j in chunks for piece in back[j]]
        return call(
            functools.partial(unpack_kernel, dims, chunks, len(extra)),
            (me, *pieces, *extra), [SMEM] + [VMEM] * len(pieces) + [HBM] * len(extra),
            jax.ShapeDtypeStruct(hidden.shape, bf16), HBM, [DMA((len(pieces),))],
            input_output_aliases={1 + len(pieces): 0} if extra else {},
        )

    result = unpack((3, 0), [unpack((1, 2), [])])
    return result, grad_tiles


def solution(mesh):
    return jax.shard_map(
        on_device,
        mesh=mesh,
        in_specs=(
            P(("groups", "seqt"), None),
            P(("groups", "seqt"), None),
            P("seqt", None, None, None),
            P(),
            P("seqt", None),
        ),
        out_specs=(P(("groups", "seqt"), None), P(("groups", "seqt"), None, None, None)),
        check_vma=False,
    )
```

```python
import functools

import jax
import jax.numpy as jnp
from jax import lax
from jax.experimental import pallas as pl
from jax.experimental.pallas import tpu as pltpu
from jax.sharding import PartitionSpec as P


PLANES = 4
TOP = 32000.0
LIMIT = 8 * 1024 * 1024
HBM = pl.BlockSpec(memory_space=pltpu.HBM)
SMEM = pl.BlockSpec(memory_space=pltpu.SMEM)
VMEM = pl.BlockSpec(memory_space=pltpu.VMEM)
DMA = pltpu.SemaphoreType.DMA


def start_all(copies, sems):
    started = []
    for n, (src, dst) in enumerate(copies):
        copy = pltpu.make_async_copy(src, dst, sems.at[n])
        copy.start()
        started.append(copy)
    return started


def wait_all(started):
    for copy in started:
        copy.wait()


def plane_of(j, z):
    even = z % 2 == 0
    if j == 0:
        return jnp.where(even, 3, 0)
    if j == 1:
        return jnp.where(z < 2, z + 2, z - 2)
    if j == 2:
        return jnp.where(even, 1, 2)
    return z


def owner(j, p, members, me_ref):
    z, m = me_ref[0] // members, me_ref[0] % members
    return plane_of(j, z) * members + (m ^ p)


def block(index, size):
    return pl.ds(pl.multiple_of(index * size, 128), size)


def pack_kernel(dims, chunks, me_ref, rows_ref, grad_ref, hidden_ref, *refs):
    members, _, cols, slots, tile = dims
    outs, sems = refs[:-1], refs[-1]
    width = cols * tile
    copies = []
    for n, j in enumerate(chunks):
        for p in range(members):
            out, who = outs[n * members + p], owner(j, p, members, me_ref)
            copies.append((hidden_ref.at[:, block(who, width)], out.at[:, pl.ds(0, width)]))
            for k in range(slots):
                copies.append((grad_ref.at[:, block(rows_ref[k, who], tile)], out.at[:, pl.ds(width + k * tile, tile)]))
    wait_all(start_all(copies, sems))


def mask_kernel(cols, slots, tile, share_ref, mask_ref, tiles_ref, own, crossing, matrix):
    for c in range(cols):
        for k in range(slots):
            factor = mask_ref[k, c].astype(jnp.float32).astype(jnp.bfloat16)
            matrix[pl.ds(c * tile, tile), pl.ds(k * tile, tile)] = tiles_ref[c, k] * factor
    quarter = cols * tile // 4
    own[pl.ds(0, quarter), :] = matrix[pl.ds(pl.multiple_of(share_ref[0] * quarter, 16), quarter), :]
    new = matrix[pl.ds(pl.multiple_of((2 + share_ref[0]) * quarter, 16), quarter), :]
    own[pl.ds(quarter, quarter), :] = new
    crossing[...] = new


def bundle_kernel(own, crossed, out):
    rows = own.shape[0]
    out[pl.ds(0, rows), :] = own[...]
    out[pl.ds(rows, crossed.shape[0]), :] = crossed[...]


def pick_kernel(members, me_ref, at_end, inside, out):
    outer = (me_ref[0] < members) | (me_ref[0] >= 3 * members)

    @pl.when(outer)
    def _():
        out[...] = at_end[...]

    @pl.when(jnp.logical_not(outer))
    def _():
        out[...] = inside[...]


def decode(ref, tiles, tile, n):
    scale = jnp.exp2(ref[pl.ds(tiles * tile + n, 1), :].astype(jnp.float32)) * (1.0 / TOP)
    return ref[pl.ds(n * tile, tile), :].astype(jnp.float32) * scale


def encode(value, out, powers, tile, n):
    top = jnp.max(jnp.abs(value), axis=0, keepdims=True)
    power = jnp.ceil(jnp.log2(jnp.maximum(top, 1e-30)))
    code = jnp.round(value * (jnp.exp2(-power) * TOP))
    out[pl.ds(n * tile, tile), :] = code.astype(jnp.int32).astype(jnp.int16)
    powers[pl.ds(n, 1), :] = power


def flush_powers(out, powers, first):
    rows = out.shape[0] - first
    out[pl.ds(first, rows), :] = powers[pl.ds(0, rows), :].astype(jnp.int32).astype(jnp.int16)


def partial_kernel(dims, pieces, *refs):
    members, tokens, cols, slots, tile = dims
    tiles, width = cols * slots, cols * tile
    parts, refs = refs[:members], refs[members:]
    outs, (picks, held, total, *powers) = refs[:max(pieces, 1)], refs[max(pieces, 1):]
    for p, part in enumerate(parts):
        rows = pl.ds(p * tokens, tokens)
        held[rows, :] = part[:, pl.ds(0, width)]
        picks[rows, :] = part[:, pl.ds(width, slots * tile)]
    total[...] = lax.dot_general(held[...], picks[...], (((0,), (0,)), ((), ())), preferred_element_type=jnp.float32)
    count = tiles // max(pieces, 1)
    for n in range(tiles):
        c, k = divmod(n, slots)
        value = total[pl.ds(c * tile, tile), pl.ds(k * tile, tile)]
        out = outs[n // count]
        if pieces:
            encode(value, out, powers[0], tile, n % count)
            if n % count == count - 1:
                flush_powers(out, powers[0], count * tile)
        else:
            out[pl.ds(n * tile, tile), :] = value


def join_kernel(tile, tiles, first, base_tiles, base, added, out, powers):
    for n in range(tiles):
        encode(decode(base, base_tiles, tile, first + n) + decode(added, tiles, tile, n), out, powers, tile, n)
    flush_powers(out, powers, tiles * tile)


def finish_kernel(dims, me_ref, mask_ref, own, out_a, out_b, inward, mid_a, mid_b, out, made, sems):
    members, _, cols, slots, tile = dims
    tiles = cols * slots
    half = tiles // 2

    def run(halves, wholes):
        writes = []
        for c in range(cols):
            for k in range(slots):
                n = c * slots + k
                value = own[pl.ds(n * tile, tile), :] + decode(halves[n // half], half, tile, n % half)
                for source in wholes:
                    value = value + decode(source, tiles, tile, n)
                made[c, k] = value * mask_ref[k, c].astype(jnp.float32)
            write = pltpu.make_async_copy(made.at[c], out.at[c], sems.at[c])
            write.start()
            writes.append(write)
        wait_all(writes)

    outer = (me_ref[0] < members) | (me_ref[0] >= 3 * members)
    pl.when(outer)(lambda: run((out_a, out_b), ()))
    pl.when(jnp.logical_not(outer))(lambda: run((mid_a, mid_b), (inward,)))


def grad_kernel(dims, chunks, me_ref, share_ref, rows_ref, *refs):
    members, _, cols, slots, tile = dims
    width, near = cols * tile, members // 2
    quarter = width // 4
    refs = list(refs)
    grads = [refs.pop(0) for _ in range(near)]
    inputs = [([refs.pop(0) for _ in range(members)], refs.pop(0), refs.pop(0)) for _ in chunks]
    olds, news, (weights, picks) = refs[:members], refs[members:members + near], refs[members + near:]

    def product(rows, n):
        made = lax.dot_general(rows, weights[n], (((1,), (1,)), ((), ())), preferred_element_type=jnp.float32)
        return made.astype(jnp.bfloat16)

    for n, j in enumerate(chunks):
        parts, mine, other = inputs[n]
        for i in range(3):
            rows = pl.ds(i * quarter, quarter)
            weights[i, pl.ds(pl.multiple_of(share_ref[0] * quarter, 16), quarter), :] = mine[rows, :]
            weights[i, pl.ds(pl.multiple_of((1 - share_ref[0]) * quarter, 16), quarter), :] = other[rows, :]
        picked = pl.ds(width, slots * tile)
        for p in range(members):
            olds[p][:, pl.ds(n * 2 * quarter, 2 * quarter)] = product(parts[p][:, picked], 0)
        across = owner(j, near, members, me_ref)
        for q in range(near):
            for k in range(slots):
                picks[:, pl.ds(k * tile, tile)] = grads[q][:, block(rows_ref[k, across], tile)]
            news[q][:, pl.ds(n * width, 2 * quarter)] = product(parts[q][:, picked], 1)
            news[q][:, pl.ds(n * width + 2 * quarter, 2 * quarter)] = product(picks[...], 2)


def unpack_kernel(dims, chunks, aliased, me_ref, *refs):
    members, _, cols, _, tile = dims
    width, near = cols * tile, members // 2
    half = width // 2
    count = members + near
    olds, news, out, sems = refs[:members], refs[members:count], refs[count + aliased], refs[-1]
    copies = []
    for n, j in enumerate(chunks):
        for p in range(members):
            who = owner(j, p, members, me_ref)
            copies.append((olds[p].at[:, pl.ds(n * half, half)], out.at[:, pl.ds(pl.multiple_of(who * width, 128), half)]))
            piece = news[p % near].at[:, pl.ds(n * width + (p // near) * half, half)]
            copies.append((piece, out.at[:, pl.ds(pl.multiple_of(who * width + half, 128), half)]))
    wait_all(start_all(copies, sems))


def on_device(out_grad, hidden, down_tiles, row_blocks, tile_mask):
    devices = lax.axis_size("seqt")
    members = devices // PLANES
    tokens = out_grad.shape[0]
    cols, slots, tile = down_tiles.shape[:3]
    width, tiles = cols * tile, cols * slots
    dims = (members, tokens, cols, slots, tile)
    scale_rows = -(-tiles // 16) * 16
    me = jnp.full((1,), lax.axis_index("seqt"), jnp.int32)
    row_blocks, tile_mask = row_blocks.T, tile_mask.T
    share = jnp.full((1,), lax.axis_index("groups") & 1, jnp.int32)
    near = members // 2
    own_grad = pltpu.with_memory_space_constraint(out_grad, pltpu.VMEM)
    out_grad, hidden = [pltpu.with_memory_space_constraint(value, pltpu.HBM) for value in (out_grad, hidden)]
    bf16, f32 = jnp.bfloat16, jnp.float32
    half = members // 2
    partners = sorted(range(1, members), key=lambda p: (p < half, p))

    def call(kernel, operands, specs, outs, out_specs, scratch, **extra):
        return pl.pallas_call(
            kernel, out_shape=outs, in_specs=specs, out_specs=out_specs, scratch_shapes=scratch,
            compiler_params=pltpu.CompilerParams(vmem_limit_bytes=LIMIT), **extra,
        )(*operands)

    def permute(value, pairs):
        return pltpu.with_memory_space_constraint(lax.ppermute(value, "seqt", pairs), pltpu.VMEM)

    def inside(value, p):
        return permute(value, [(i, i ^ p) for i in range(devices)])

    def over_x(value):
        moved = lax.ppermute(value, "groups", [(i, i ^ 1) for i in range(lax.axis_size("groups"))])
        return pltpu.with_memory_space_constraint(moved, pltpu.VMEM)

    def across(value, pairs):
        return permute(value, [(a * members + i, b * members + i) for a, b in pairs for i in range(members)])

    parts = [None] * PLANES
    for chunks in ((0,), (1, 2, 3)):
        count = len(chunks) * members
        packed = call(
            functools.partial(pack_kernel, dims, chunks),
            (me, row_blocks, out_grad, hidden), [SMEM, SMEM, HBM, HBM],
            [pltpu.VMEM((tokens, width + slots * tile), bf16)] * count,
            [VMEM] * count, [DMA((count * (slots + 1),))],
        )
        for n, j in enumerate(chunks):
            mine = packed[n * members:(n + 1) * members]
            arrived = {p: inside(mine[p], p) for p in partners}
            parts[j] = [mine[0]] + [arrived[p] for p in range(1, members)]

    grads = [own_grad] + [inside(out_grad, q) for q in range(1, near)]

    depth, quarter = slots * tile, width // 4
    own_rows, crossing = call(
        functools.partial(mask_kernel, cols, slots, tile), (share, tile_mask, down_tiles), [SMEM, SMEM, VMEM],
        [pltpu.VMEM((2 * quarter, depth), bf16), pltpu.VMEM((quarter, depth), bf16)], [VMEM, VMEM],
        [pltpu.VMEM((width, depth), bf16)],
    )
    bundle = call(
        bundle_kernel, (own_rows, inside(crossing, near)), [VMEM, VMEM],
        pltpu.VMEM((3 * quarter, depth), bf16), VMEM, [],
    )
    pairs, inward, middle, outward = [(0, 1), (1, 0), (2, 3), (3, 2)], [(0, 1), (3, 2)], [(1, 2), (2, 1)], [(1, 0), (2, 3)]
    e1, m1 = across(bundle, pairs), across(bundle, middle)
    m2, o1 = across(e1, middle), across(m1, outward)
    o2 = across(m2, outward)

    def pick(at_end, inner):
        return call(
            functools.partial(pick_kernel, members), (me, at_end, inner), [SMEM, VMEM, VMEM],
            pltpu.VMEM((3 * quarter, depth), bf16), VMEM, [],
        )

    shares = {3: bundle, 2: pick(e1, m1), 1: pick(o1, m2), 0: pick(o2, e1)}
    others = {j: over_x(value) for j, value in shares.items()}

    def coded(count):
        return pltpu.VMEM((count * tile + -(-count // 16) * 16, tile), jnp.int16)

    half = tiles // 2
    powers = pltpu.VMEM((scale_rows, tile), f32)

    def partial(j, pieces):
        outs = [coded(tiles // pieces)] * pieces if pieces else [pltpu.VMEM((tiles * tile, tile), f32)]
        return call(
            functools.partial(partial_kernel, dims, pieces), parts[j], [VMEM] * members,
            outs, [VMEM] * len(outs),
            [
                pltpu.VMEM((members * tokens, slots * tile), bf16),
                pltpu.VMEM((members * tokens, width), bf16),
                pltpu.VMEM((width, slots * tile), f32),
            ] + ([powers] if pieces else []),
        )

    def give_back(chunks):
        count = len(chunks)
        operands = [me, share, row_blocks, *grads]
        for j in chunks:
            operands += [*parts[j], shares[j], others[j]]
        products = call(
            functools.partial(grad_kernel, dims, chunks),
            operands, [SMEM] * 3 + [VMEM] * (len(operands) - 3),
            [pltpu.VMEM((tokens, count * 2 * quarter), bf16)] * members + [pltpu.VMEM((tokens, count * width), bf16)] * near,
            [VMEM] * (members + near),
            [pltpu.VMEM((3, 2 * quarter, depth), bf16), pltpu.VMEM((tokens, depth), bf16)],
        )
        arrived = {p: inside(products[p], p) for p in partners}
        olds = [products[0]] + [arrived[p] for p in range(1, members)]
        news = [products[members]] + [inside(products[members + q], q) for q in range(1, near)]
        return olds + news

    def join(base, base_tiles, first, added):
        return call(
            functools.partial(join_kernel, tile, half, first, base_tiles), (base, added), [VMEM, VMEM],
            coded(half), VMEM, [powers],
        )

    halves = range(2)
    sums_0, sums_1, (sums_2,), (own,) = partial(0, 2), partial(1, 2), partial(2, 1), partial(3, 0)
    i1 = [across(sums_0[n], inward) for n in halves]
    i2 = [across(sums_1[n], inward) for n in halves]
    i3 = across(sums_2, inward)
    x1 = [across(join(sums_1[n], half, 0, i1[n]), middle) for n in halves]
    x2 = [across(join(sums_2, tiles, n * half, i2[n]), middle) for n in halves]
    last = [across(join(sums_0[n], half, 0, x1[n]), outward) for n in halves]

    sets = {"a": (2,), "b": (1, 3), "c": (0,)}
    back = {name: give_back(chunks) for name, chunks in sets.items()}

    grad_tiles = call(
        functools.partial(finish_kernel, dims), (me, tile_mask, own, *last, i3, *x2),
        [SMEM, SMEM] + [VMEM] * 6, jax.ShapeDtypeStruct((cols, slots, tile, tile), f32), HBM,
        [pltpu.VMEM((cols, slots, tile, tile), f32), DMA((cols,))],
    )

    def unpack(chunks, pieces, extra):
        return call(
            functools.partial(unpack_kernel, dims, chunks, len(extra)),
            (me, *pieces, *extra), [SMEM] + [VMEM] * len(pieces) + [HBM] * len(extra),
            jax.ShapeDtypeStruct(hidden.shape, bf16), HBM, [DMA((2 * members * len(chunks),))],
            input_output_aliases={1 + len(pieces): 0} if extra else {},
        )

    result = []
    for name, chunks in sets.items():
        result = [unpack(chunks, back[name], result)]
    return result[0], grad_tiles


def solution(mesh):
    return jax.shard_map(
        on_device,
        mesh=mesh,
        in_specs=(
            P(("groups", "seqt"), None),
            P(("groups", "seqt"), None),
            P("seqt", None, None, None),
            P(),
            P("seqt", None),
        ),
        out_specs=(P(("groups", "seqt"), None), P(("groups", "seqt"), None, None, None)),
        check_vma=False,
    )
```

```python
import functools

import jax
import jax.numpy as jnp
from jax import lax
from jax.experimental import pallas as pl
from jax.experimental.pallas import tpu as pltpu
from jax.sharding import PartitionSpec as P


PLANES = 4
TOP = 32000.0
LIMIT = 8 * 1024 * 1024
HBM = pl.BlockSpec(memory_space=pltpu.HBM)
SMEM = pl.BlockSpec(memory_space=pltpu.SMEM)
VMEM = pl.BlockSpec(memory_space=pltpu.VMEM)
DMA = pltpu.SemaphoreType.DMA


def start_all(copies, sems):
    started = []
    for n, (src, dst) in enumerate(copies):
        copy = pltpu.make_async_copy(src, dst, sems.at[n])
        copy.start()
        started.append(copy)
    return started


def wait_all(started):
    for copy in started:
        copy.wait()


def plane_of(j, z):
    even = z % 2 == 0
    if j == 0:
        return jnp.where(even, 3, 0)
    if j == 1:
        return jnp.where(z < 2, z + 2, z - 2)
    if j == 2:
        return jnp.where(even, 1, 2)
    return z


def owner(j, p, members, me_ref):
    z, m = me_ref[0] // members, me_ref[0] % members
    return plane_of(j, z) * members + (m ^ p)


def block(index, size):
    return pl.ds(pl.multiple_of(index * size, 128), size)


def pack_kernel(dims, chunks, me_ref, rows_ref, grad_ref, hidden_ref, *refs):
    members, _, cols, slots, tile = dims
    outs, sems = refs[:-1], refs[-1]
    width = cols * tile
    copies = []
    for n, j in enumerate(chunks):
        for p in range(members):
            out, who = outs[n * members + p], owner(j, p, members, me_ref)
            copies.append((hidden_ref.at[:, block(who, width)], out.at[:, pl.ds(0, width)]))
            for k in range(slots):
                copies.append((grad_ref.at[:, block(rows_ref[k, who], tile)], out.at[:, pl.ds(width + k * tile, tile)]))
    wait_all(start_all(copies, sems))


def mask_kernel(cols, slots, tile, share_ref, mask_ref, tiles_ref, own, crossing, matrix):
    for c in range(cols):
        for k in range(slots):
            factor = mask_ref[k, c].astype(jnp.float32).astype(jnp.bfloat16)
            matrix[pl.ds(c * tile, tile), pl.ds(k * tile, tile)] = tiles_ref[c, k] * factor
    quarter = cols * tile // 4
    own[pl.ds(0, quarter), :] = matrix[pl.ds(pl.multiple_of(share_ref[0] * quarter, 16), quarter), :]
    new = matrix[pl.ds(pl.multiple_of((2 + share_ref[0]) * quarter, 16), quarter), :]
    own[pl.ds(quarter, quarter), :] = new
    crossing[...] = new


def bundle_kernel(own, crossed, out):
    rows = own.shape[0]
    out[pl.ds(0, rows), :] = own[...]
    out[pl.ds(rows, crossed.shape[0]), :] = crossed[...]


def pick_kernel(members, me_ref, at_end, inside, out):
    outer = (me_ref[0] < members) | (me_ref[0] >= 3 * members)

    @pl.when(outer)
    def _():
        out[...] = at_end[...]

    @pl.when(jnp.logical_not(outer))
    def _():
        out[...] = inside[...]


def decode(ref, tiles, tile, n):
    scale = jnp.exp2(ref[pl.ds(tiles * tile + n, 1), :].astype(jnp.float32)) * (1.0 / TOP)
    return ref[pl.ds(n * tile, tile), :].astype(jnp.float32) * scale


def encode(value, out, powers, tile, n):
    top = jnp.max(jnp.abs(value), axis=0, keepdims=True)
    power = jnp.ceil(jnp.log2(jnp.maximum(top, 1e-30)))
    code = jnp.round(value * (jnp.exp2(-power) * TOP))
    out[pl.ds(n * tile, tile), :] = code.astype(jnp.int32).astype(jnp.int16)
    powers[pl.ds(n, 1), :] = power


def flush_powers(out, powers, first):
    rows = out.shape[0] - first
    out[pl.ds(first, rows), :] = powers[pl.ds(0, rows), :].astype(jnp.int32).astype(jnp.int16)


def partial_kernel(dims, pieces, *refs):
    members, tokens, cols, slots, tile = dims
    tiles, width = cols * slots, cols * tile
    parts, refs = refs[:members], refs[members:]
    outs, (picks, held, total, *powers) = refs[:max(pieces, 1)], refs[max(pieces, 1):]
    for p, part in enumerate(parts):
        rows = pl.ds(p * tokens, tokens)
        held[rows, :] = part[:, pl.ds(0, width)]
        picks[rows, :] = part[:, pl.ds(width, slots * tile)]
    total[...] = lax.dot_general(held[...], picks[...], (((0,), (0,)), ((), ())), preferred_element_type=jnp.float32)
    count = tiles // max(pieces, 1)
    for n in range(tiles):
        c, k = divmod(n, slots)
        value = total[pl.ds(c * tile, tile), pl.ds(k * tile, tile)]
        out = outs[n // count]
        if pieces:
            encode(value, out, powers[0], tile, n % count)
            if n % count == count - 1:
                flush_powers(out, powers[0], count * tile)
        else:
            out[pl.ds(n * tile, tile), :] = value


def join_kernel(tile, tiles, first, base_tiles, base, added, out, powers):
    for n in range(tiles):
        encode(decode(base, base_tiles, tile, first + n) + decode(added, tiles, tile, n), out, powers, tile, n)
    flush_powers(out, powers, tiles * tile)


def finish_tiles(dims, part, me_ref, mask_ref, own, outward, inward, middle, out, made, sems):
    members, _, cols, slots, tile = dims
    half = cols * slots // 2
    columns = range(part * cols // 2, (part + 1) * cols // 2)
    writes = [pltpu.make_async_copy(made.at[c - columns[0]], out.at[c], sems.at[c - columns[0]]) for c in columns]

    def run(with_halves, wholes):
        for c, write in zip(columns, writes):
            for k in range(slots):
                n = c * slots + k
                value = own[pl.ds(n * tile, tile), :] + decode(with_halves, half, tile, n % half)
                for source in wholes:
                    value = value + decode(source, 2 * half, tile, n)
                made[c - columns[0], k] = value * mask_ref[k, c].astype(jnp.float32)
            write.start()

    outer = (me_ref[0] < members) | (me_ref[0] >= 3 * members)
    pl.when(outer)(lambda: run(outward, ()))
    pl.when(jnp.logical_not(outer))(lambda: run(middle, (inward,)))
    return writes


def finish_kernel(dims, *refs):
    wait_all(finish_tiles(dims, 0, *refs))


def final_kernel(dims, chunks, me_ref, mask_ref, own, outward, inward, middle, *refs):
    members = dims[0]
    count = members + members // 2
    pieces, (result, tiles_out, made, tile_sems, sems) = refs[:count], refs[count + 2:]
    started = start_all(unpack_copies(dims, chunks, me_ref, pieces, result), sems)
    wait_all(finish_tiles(dims, 1, me_ref, mask_ref, own, outward, inward, middle, tiles_out, made, tile_sems) + started)


def grad_kernel(dims, chunks, me_ref, share_ref, rows_ref, *refs):
    members, _, cols, slots, tile = dims
    width, near = cols * tile, members // 2
    quarter = width // 4
    refs = list(refs)
    grads = [refs.pop(0) for _ in range(near)]
    inputs = [([refs.pop(0) for _ in range(members)], refs.pop(0), refs.pop(0)) for _ in chunks]
    olds, news, (weights, picks) = refs[:members], refs[members:members + near], refs[members + near:]

    def product(rows, n):
        made = lax.dot_general(rows, weights[n], (((1,), (1,)), ((), ())), preferred_element_type=jnp.float32)
        return made.astype(jnp.bfloat16)

    for n, j in enumerate(chunks):
        parts, mine, other = inputs[n]
        for i in range(3):
            rows = pl.ds(i * quarter, quarter)
            weights[i, pl.ds(pl.multiple_of(share_ref[0] * quarter, 16), quarter), :] = mine[rows, :]
            weights[i, pl.ds(pl.multiple_of((1 - share_ref[0]) * quarter, 16), quarter), :] = other[rows, :]
        picked = pl.ds(width, slots * tile)
        for p in range(members):
            olds[p][:, pl.ds(n * 2 * quarter, 2 * quarter)] = product(parts[p][:, picked], 0)
        across = owner(j, near, members, me_ref)
        for q in range(near):
            for k in range(slots):
                picks[:, pl.ds(k * tile, tile)] = grads[q][:, block(rows_ref[k, across], tile)]
            news[q][:, pl.ds(n * width, 2 * quarter)] = product(parts[q][:, picked], 1)
            news[q][:, pl.ds(n * width + 2 * quarter, 2 * quarter)] = product(picks[...], 2)


def unpack_copies(dims, chunks, me_ref, pieces, out):
    members, _, cols, _, tile = dims
    width, near = cols * tile, members // 2
    half = width // 2
    olds, news = pieces[:members], pieces[members:]
    copies = []
    for n, j in enumerate(chunks):
        for p in range(members):
            who = owner(j, p, members, me_ref)
            copies.append((olds[p].at[:, pl.ds(n * half, half)], out.at[:, pl.ds(pl.multiple_of(who * width, 128), half)]))
            piece = news[p % near].at[:, pl.ds(n * width + (p // near) * half, half)]
            copies.append((piece, out.at[:, pl.ds(pl.multiple_of(who * width + half, 128), half)]))
    return copies


def unpack_kernel(dims, chunks, aliased, me_ref, *refs):
    count = dims[0] + dims[0] // 2
    wait_all(start_all(unpack_copies(dims, chunks, me_ref, refs[:count], refs[count + aliased]), refs[-1]))


def on_device(out_grad, hidden, down_tiles, row_blocks, tile_mask):
    devices = lax.axis_size("seqt")
    members = devices // PLANES
    tokens = out_grad.shape[0]
    cols, slots, tile = down_tiles.shape[:3]
    width, tiles = cols * tile, cols * slots
    dims = (members, tokens, cols, slots, tile)
    scale_rows = -(-tiles // 16) * 16
    me = jnp.full((1,), lax.axis_index("seqt"), jnp.int32)
    row_blocks, tile_mask = [pltpu.with_memory_space_constraint(value.T, pltpu.HBM) for value in (row_blocks, tile_mask)]
    share = jnp.full((1,), lax.axis_index("groups") & 1, jnp.int32)
    near = members // 2
    own_grad = pltpu.with_memory_space_constraint(out_grad, pltpu.VMEM)
    out_grad, hidden = [pltpu.with_memory_space_constraint(value, pltpu.HBM) for value in (out_grad, hidden)]
    bf16, f32 = jnp.bfloat16, jnp.float32
    half = members // 2
    partners = sorted(range(1, members), key=lambda p: (p < half, p))

    def call(kernel, operands, specs, outs, out_specs, scratch, **extra):
        return pl.pallas_call(
            kernel, out_shape=outs, in_specs=specs, out_specs=out_specs, scratch_shapes=scratch,
            compiler_params=pltpu.CompilerParams(vmem_limit_bytes=LIMIT), **extra,
        )(*operands)

    def permute(value, pairs):
        return pltpu.with_memory_space_constraint(lax.ppermute(value, "seqt", pairs), pltpu.VMEM)

    def inside(value, p):
        return permute(value, [(i, i ^ p) for i in range(devices)])

    def over_x(value):
        moved = lax.ppermute(value, "groups", [(i, i ^ 1) for i in range(lax.axis_size("groups"))])
        return pltpu.with_memory_space_constraint(moved, pltpu.VMEM)

    def across(value, pairs):
        return permute(value, [(a * members + i, b * members + i) for a, b in pairs for i in range(members)])

    parts = [None] * PLANES
    for chunks in ((0,), (1, 2, 3)):
        count = len(chunks) * members
        packed = call(
            functools.partial(pack_kernel, dims, chunks),
            (me, row_blocks, out_grad, hidden), [SMEM, SMEM, HBM, HBM],
            [pltpu.VMEM((tokens, width + slots * tile), bf16)] * count,
            [VMEM] * count, [DMA((count * (slots + 1),))],
        )
        for n, j in enumerate(chunks):
            mine = packed[n * members:(n + 1) * members]
            arrived = {p: inside(mine[p], p) for p in partners}
            parts[j] = [mine[0]] + [arrived[p] for p in range(1, members)]

    grads = [own_grad] + [inside(out_grad, q) for q in range(1, near)]

    depth, quarter = slots * tile, width // 4
    own_rows, crossing = call(
        functools.partial(mask_kernel, cols, slots, tile), (share, tile_mask, down_tiles), [SMEM, SMEM, VMEM],
        [pltpu.VMEM((2 * quarter, depth), bf16), pltpu.VMEM((quarter, depth), bf16)], [VMEM, VMEM],
        [pltpu.VMEM((width, depth), bf16)],
    )
    bundle = call(
        bundle_kernel, (own_rows, inside(crossing, near)), [VMEM, VMEM],
        pltpu.VMEM((3 * quarter, depth), bf16), VMEM, [],
    )
    pairs, inward, middle, outward = [(0, 1), (1, 0), (2, 3), (3, 2)], [(0, 1), (3, 2)], [(1, 2), (2, 1)], [(1, 0), (2, 3)]
    e1, m1 = across(bundle, pairs), across(bundle, middle)
    m2, o1 = across(e1, middle), across(m1, outward)
    o2 = across(m2, outward)

    def pick(at_end, inner):
        return call(
            functools.partial(pick_kernel, members), (me, at_end, inner), [SMEM, VMEM, VMEM],
            pltpu.VMEM((3 * quarter, depth), bf16), VMEM, [],
        )

    shares = {3: bundle, 2: pick(e1, m1), 1: pick(o1, m2), 0: pick(o2, e1)}
    others = {j: over_x(value) for j, value in shares.items()}

    def coded(count):
        return pltpu.VMEM((count * tile + -(-count // 16) * 16, tile), jnp.int16)

    half = tiles // 2
    powers = pltpu.VMEM((scale_rows, tile), f32)

    def partial(j, pieces):
        outs = [coded(tiles // pieces)] * pieces if pieces else [pltpu.VMEM((tiles * tile, tile), f32)]
        return call(
            functools.partial(partial_kernel, dims, pieces), parts[j], [VMEM] * members,
            outs, [VMEM] * len(outs),
            [
                pltpu.VMEM((members * tokens, slots * tile), bf16),
                pltpu.VMEM((members * tokens, width), bf16),
                pltpu.VMEM((width, slots * tile), f32),
            ] + ([powers] if pieces else []),
        )

    def give_back(chunks):
        count = len(chunks)
        operands = [me, share, row_blocks, *grads]
        for j in chunks:
            operands += [*parts[j], shares[j], others[j]]
        products = call(
            functools.partial(grad_kernel, dims, chunks),
            operands, [SMEM] * 3 + [VMEM] * (len(operands) - 3),
            [pltpu.VMEM((tokens, count * 2 * quarter), bf16)] * members + [pltpu.VMEM((tokens, count * width), bf16)] * near,
            [VMEM] * (members + near),
            [pltpu.VMEM((3, 2 * quarter, depth), bf16), pltpu.VMEM((tokens, depth), bf16)],
        )
        arrived = {p: inside(products[p], p) for p in partners}
        olds = [products[0]] + [arrived[p] for p in range(1, members)]
        news = [products[members]] + [inside(products[members + q], q) for q in range(1, near)]
        return olds + news

    def join(base, base_tiles, first, added):
        return call(
            functools.partial(join_kernel, tile, half, first, base_tiles), (base, added), [VMEM, VMEM],
            coded(half), VMEM, [powers],
        )

    halves = range(2)
    sums_0, sums_1, (sums_2,), (own,) = partial(0, 2), partial(1, 2), partial(2, 1), partial(3, 0)
    i1 = [across(sums_0[n], inward) for n in halves]
    i2 = [across(sums_1[n], inward) for n in halves]
    i3 = across(sums_2, inward)
    x1 = [across(join(sums_1[n], half, 0, i1[n]), middle) for n in halves]
    x2 = [across(join(sums_2, tiles, n * half, i2[n]), middle) for n in halves]
    last = [across(join(sums_0[n], half, 0, x1[n]), outward) for n in halves]

    sets = {"a": (2,), "b": (1, 3), "c": (0,)}
    back = {name: give_back(chunks) for name, chunks in sets.items()}

    tiles_shape = jax.ShapeDtypeStruct((cols, slots, tile, tile), f32)
    made = pltpu.VMEM((cols // 2, slots, tile, tile), f32)
    grad_tiles = call(
        functools.partial(finish_kernel, dims), (me, tile_mask, own, last[0], i3, x2[0]),
        [SMEM, SMEM] + [VMEM] * 4, tiles_shape, HBM, [made, DMA((cols // 2,))],
    )

    def unpack(chunks, pieces, extra):
        return call(
            functools.partial(unpack_kernel, dims, chunks, len(extra)),
            (me, *pieces, *extra), [SMEM] + [VMEM] * len(pieces) + [HBM] * len(extra),
            jax.ShapeDtypeStruct(hidden.shape, bf16), HBM, [DMA((2 * members * len(chunks),))],
            input_output_aliases={1 + len(pieces): 0} if extra else {},
        )

    result = unpack(sets["b"], back["b"], [unpack(sets["a"], back["a"], [])])
    pieces = back["c"]
    return call(
        functools.partial(final_kernel, dims, sets["c"]),
        (me, tile_mask, own, last[1], i3, x2[1], *pieces, result, grad_tiles),
        [SMEM, SMEM] + [VMEM] * (4 + len(pieces)) + [HBM, HBM],
        [jax.ShapeDtypeStruct(hidden.shape, bf16), tiles_shape], [HBM, HBM],
        [made, DMA((cols // 2,)), DMA((2 * members,))],
        input_output_aliases={6 + len(pieces): 0, 7 + len(pieces): 1},
    )


def solution(mesh):
    return jax.shard_map(
        on_device,
        mesh=mesh,
        in_specs=(
            P(("groups", "seqt"), None),
            P(("groups", "seqt"), None),
            P("seqt", None, None, None),
            P(),
            P("seqt", None),
        ),
        out_specs=(P(("groups", "seqt"), None), P(("groups", "seqt"), None, None, None)),
        check_vma=False,
    )
```

```python
import functools

import jax
import jax.numpy as jnp
from jax import lax
from jax.experimental import pallas as pl
from jax.experimental.pallas import tpu as pltpu
from jax.sharding import PartitionSpec as P


PLANES = 4
TOP = 32000.0
LIMIT = 8 * 1024 * 1024
HBM = pl.BlockSpec(memory_space=pltpu.HBM)
SMEM = pl.BlockSpec(memory_space=pltpu.SMEM)
VMEM = pl.BlockSpec(memory_space=pltpu.VMEM)
DMA = pltpu.SemaphoreType.DMA


def start_all(copies, sems):
    started = []
    for n, (src, dst) in enumerate(copies):
        copy = pltpu.make_async_copy(src, dst, sems.at[n])
        copy.start()
        started.append(copy)
    return started


def wait_all(started):
    for copy in started:
        copy.wait()


def plane_of(j, z):
    even = z % 2 == 0
    if j == 0:
        return jnp.where(even, 3, 0)
    if j == 1:
        return jnp.where(z < 2, z + 2, z - 2)
    if j == 2:
        return jnp.where(even, 1, 2)
    return z


def owner(j, p, members, me_ref):
    z, m = me_ref[0] // members, me_ref[0] % members
    return plane_of(j, z) * members + (m ^ p)


def block(index, size):
    return pl.ds(pl.multiple_of(index * size, 128), size)


def pack_kernel(dims, chunks, me_ref, rows_ref, grad_ref, hidden_ref, *refs):
    members, _, cols, slots, tile = dims
    outs, sems = refs[:-1], refs[-1]
    width = cols * tile
    copies = []
    for n, j in enumerate(chunks):
        for p in range(members):
            out, who = outs[n * members + p], owner(j, p, members, me_ref)
            copies.append((hidden_ref.at[:, block(who, width)], out.at[:, pl.ds(0, width)]))
            for k in range(slots):
                copies.append((grad_ref.at[:, block(rows_ref[k, who], tile)], out.at[:, pl.ds(width + k * tile, tile)]))
    wait_all(start_all(copies, sems))


def mask_kernel(cols, slots, tile, share_ref, mask_ref, tiles_ref, own, crossing, matrix):
    for c in range(cols):
        for k in range(slots):
            factor = mask_ref[k, c].astype(jnp.float32).astype(jnp.bfloat16)
            matrix[pl.ds(c * tile, tile), pl.ds(k * tile, tile)] = tiles_ref[c, k] * factor
    quarter = cols * tile // 4
    own[pl.ds(0, quarter), :] = matrix[pl.ds(pl.multiple_of(share_ref[0] * quarter, 16), quarter), :]
    new = matrix[pl.ds(pl.multiple_of((2 + share_ref[0]) * quarter, 16), quarter), :]
    own[pl.ds(quarter, quarter), :] = new
    crossing[...] = new


def bundle_kernel(own, crossed, out):
    rows = own.shape[0]
    out[pl.ds(0, rows), :] = own[...]
    out[pl.ds(rows, crossed.shape[0]), :] = crossed[...]


def pick_kernel(members, me_ref, at_end, inside, out):
    outer = (me_ref[0] < members) | (me_ref[0] >= 3 * members)

    @pl.when(outer)
    def _():
        out[...] = at_end[...]

    @pl.when(jnp.logical_not(outer))
    def _():
        out[...] = inside[...]


def decode(ref, tiles, tile, n):
    scale = jnp.exp2(ref[pl.ds(tiles * tile + n, 1), :].astype(jnp.float32)) * (1.0 / TOP)
    return ref[pl.ds(n * tile, tile), :].astype(jnp.float32) * scale


def encode(value, out, powers, tile, n):
    top = jnp.max(jnp.abs(value), axis=0, keepdims=True)
    power = jnp.ceil(jnp.log2(jnp.maximum(top, 1e-30)))
    code = jnp.round(value * (jnp.exp2(-power) * TOP))
    out[pl.ds(n * tile, tile), :] = code.astype(jnp.int32).astype(jnp.int16)
    powers[pl.ds(n, 1), :] = power


def flush_powers(out, powers, first):
    rows = out.shape[0] - first
    out[pl.ds(first, rows), :] = powers[pl.ds(0, rows), :].astype(jnp.int32).astype(jnp.int16)


def partial_kernel(dims, pieces, *refs):
    members, tokens, cols, slots, tile = dims
    tiles, width = cols * slots, cols * tile
    parts, refs = refs[:members], refs[members:]
    outs, (picks, held, total, *powers) = refs[:max(pieces, 1)], refs[max(pieces, 1):]
    for p, part in enumerate(parts):
        rows = pl.ds(p * tokens, tokens)
        held[rows, :] = part[:, pl.ds(0, width)]
        picks[rows, :] = part[:, pl.ds(width, slots * tile)]
    total[...] = lax.dot_general(held[...], picks[...], (((0,), (0,)), ((), ())), preferred_element_type=jnp.float32)
    count = tiles // max(pieces, 1)
    for n in range(tiles):
        c, k = divmod(n, slots)
        value = total[pl.ds(c * tile, tile), pl.ds(k * tile, tile)]
        out = outs[n // count]
        if pieces:
            encode(value, out, powers[0], tile, n % count)
            if n % count == count - 1:
                flush_powers(out, powers[0], count * tile)
        else:
            out[pl.ds(n * tile, tile), :] = value


def join_kernel(tile, tiles, first, base_tiles, base, added, out, powers):
    for n in range(tiles):
        encode(decode(base, base_tiles, tile, first + n) + decode(added, tiles, tile, n), out, powers, tile, n)
    flush_powers(out, powers, tiles * tile)


def finish_kernel(dims, me_ref, mask_ref, own, out_a, out_b, inward, mid_a, mid_b, out, made, sems):
    members, _, cols, slots, tile = dims
    tiles = cols * slots
    half = tiles // 2

    def run(halves, wholes):
        writes = []
        for c in range(cols):
            for k in range(slots):
                n = c * slots + k
                value = own[pl.ds(n * tile, tile), :] + decode(halves[n // half], half, tile, n % half)
                for source in wholes:
                    value = value + decode(source, tiles, tile, n)
                made[c, k] = value * mask_ref[k, c].astype(jnp.float32)
            write = pltpu.make_async_copy(made.at[c], out.at[c], sems.at[c])
            write.start()
            writes.append(write)
        wait_all(writes)

    outer = (me_ref[0] < members) | (me_ref[0] >= 3 * members)
    pl.when(outer)(lambda: run((out_a, out_b), ()))
    pl.when(jnp.logical_not(outer))(lambda: run((mid_a, mid_b), (inward,)))


def grad_kernel(dims, chunks, me_ref, share_ref, rows_ref, *refs):
    members, _, cols, slots, tile = dims
    width, near = cols * tile, members // 2
    quarter = width // 4
    refs = list(refs)
    grads = [refs.pop(0) for _ in range(near)]
    inputs = [([refs.pop(0) for _ in range(members)], refs.pop(0), refs.pop(0)) for _ in chunks]
    olds, news, (weights, picks) = refs[:members], refs[members:members + near], refs[members + near:]

    def product(rows, n):
        made = lax.dot_general(rows, weights[n], (((1,), (1,)), ((), ())), preferred_element_type=jnp.float32)
        return made.astype(jnp.bfloat16)

    for n, j in enumerate(chunks):
        parts, mine, other = inputs[n]
        for i in range(3):
            rows = pl.ds(i * quarter, quarter)
            weights[i, pl.ds(pl.multiple_of(share_ref[0] * quarter, 16), quarter), :] = mine[rows, :]
            weights[i, pl.ds(pl.multiple_of((1 - share_ref[0]) * quarter, 16), quarter), :] = other[rows, :]
        picked = pl.ds(width, slots * tile)
        for p in range(members):
            olds[p][:, pl.ds(n * 2 * quarter, 2 * quarter)] = product(parts[p][:, picked], 0)
        across = owner(j, near, members, me_ref)
        for q in range(near):
            for k in range(slots):
                picks[:, pl.ds(k * tile, tile)] = grads[q][:, block(rows_ref[k, across], tile)]
            news[q][:, pl.ds(n * width, 2 * quarter)] = product(parts[q][:, picked], 1)
            news[q][:, pl.ds(n * width + 2 * quarter, 2 * quarter)] = product(picks[...], 2)


def unpack_kernel(dims, chunks, aliased, me_ref, *refs):
    members, _, cols, _, tile = dims
    width, near = cols * tile, members // 2
    half = width // 2
    count = members + near
    olds, news, out, sems = refs[:members], refs[members:count], refs[count + aliased], refs[-1]
    copies = []
    for n, j in enumerate(chunks):
        for p in range(members):
            who = owner(j, p, members, me_ref)
            copies.append((olds[p].at[:, pl.ds(n * half, half)], out.at[:, pl.ds(pl.multiple_of(who * width, 128), half)]))
            piece = news[p % near].at[:, pl.ds(n * width + (p // near) * half, half)]
            copies.append((piece, out.at[:, pl.ds(pl.multiple_of(who * width + half, 128), half)]))
    wait_all(start_all(copies, sems))


def on_device(out_grad, hidden, down_tiles, row_blocks, tile_mask):
    devices = lax.axis_size("seqt")
    members = devices // PLANES
    tokens = out_grad.shape[0]
    cols, slots, tile = down_tiles.shape[:3]
    width, tiles = cols * tile, cols * slots
    dims = (members, tokens, cols, slots, tile)
    scale_rows = -(-tiles // 16) * 16
    me = jnp.full((1,), lax.axis_index("seqt"), jnp.int32)
    row_blocks, tile_mask = row_blocks.T, tile_mask.T
    rows_early, mask_early = [pltpu.with_memory_space_constraint(value, pltpu.HBM) for value in (row_blocks, tile_mask)]
    share = jnp.full((1,), lax.axis_index("groups") & 1, jnp.int32)
    near = members // 2
    own_grad = pltpu.with_memory_space_constraint(out_grad, pltpu.VMEM)
    out_grad, hidden = [pltpu.with_memory_space_constraint(value, pltpu.HBM) for value in (out_grad, hidden)]
    bf16, f32 = jnp.bfloat16, jnp.float32
    half = members // 2
    partners = sorted(range(1, members), key=lambda p: (p < half, p))

    def call(kernel, operands, specs, outs, out_specs, scratch, **extra):
        return pl.pallas_call(
            kernel, out_shape=outs, in_specs=specs, out_specs=out_specs, scratch_shapes=scratch,
            compiler_params=pltpu.CompilerParams(vmem_limit_bytes=LIMIT), **extra,
        )(*operands)

    def permute(value, pairs):
        return pltpu.with_memory_space_constraint(lax.ppermute(value, "seqt", pairs), pltpu.VMEM)

    def inside(value, p):
        return permute(value, [(i, i ^ p) for i in range(devices)])

    def over_x(value):
        moved = lax.ppermute(value, "groups", [(i, i ^ 1) for i in range(lax.axis_size("groups"))])
        return pltpu.with_memory_space_constraint(moved, pltpu.VMEM)

    def across(value, pairs):
        return permute(value, [(a * members + i, b * members + i) for a, b in pairs for i in range(members)])

    parts = [None] * PLANES
    for chunks in ((0,), (1, 2, 3)):
        count = len(chunks) * members
        packed = call(
            functools.partial(pack_kernel, dims, chunks),
            (me, rows_early, out_grad, hidden), [SMEM, SMEM, HBM, HBM],
            [pltpu.VMEM((tokens, width + slots * tile), bf16)] * count,
            [VMEM] * count, [DMA((count * (slots + 1),))],
        )
        for n, j in enumerate(chunks):
            mine = packed[n * members:(n + 1) * members]
            arrived = {p: inside(mine[p], p) for p in partners}
            parts[j] = [mine[0]] + [arrived[p] for p in range(1, members)]

    grads = [own_grad] + [inside(out_grad, q) for q in range(1, near)]

    depth, quarter = slots * tile, width // 4
    own_rows, crossing = call(
        functools.partial(mask_kernel, cols, slots, tile), (share, mask_early, down_tiles), [SMEM, SMEM, VMEM],
        [pltpu.VMEM((2 * quarter, depth), bf16), pltpu.VMEM((quarter, depth), bf16)], [VMEM, VMEM],
        [pltpu.VMEM((width, depth), bf16)],
    )
    bundle = call(
        bundle_kernel, (own_rows, inside(crossing, near)), [VMEM, VMEM],
        pltpu.VMEM((3 * quarter, depth), bf16), VMEM, [],
    )
    pairs, inward, middle, outward = [(0, 1), (1, 0), (2, 3), (3, 2)], [(0, 1), (3, 2)], [(1, 2), (2, 1)], [(1, 0), (2, 3)]
    e1, m1 = across(bundle, pairs), across(bundle, middle)
    m2, o1 = across(e1, middle), across(m1, outward)
    o2 = across(m2, outward)

    def pick(at_end, inner):
        return call(
            functools.partial(pick_kernel, members), (me, at_end, inner), [SMEM, VMEM, VMEM],
            pltpu.VMEM((3 * quarter, depth), bf16), VMEM, [],
        )

    shares = {3: bundle, 2: pick(e1, m1), 1: pick(o1, m2), 0: pick(o2, e1)}
    others = {j: over_x(value) for j, value in shares.items()}

    def coded(count):
        return pltpu.VMEM((count * tile + -(-count // 16) * 16, tile), jnp.int16)

    half = tiles // 2
    powers = pltpu.VMEM((scale_rows, tile), f32)

    def partial(j, pieces):
        outs = [coded(tiles // pieces)] * pieces if pieces else [pltpu.VMEM((tiles * tile, tile), f32)]
        return call(
            functools.partial(partial_kernel, dims, pieces), parts[j], [VMEM] * members,
            outs, [VMEM] * len(outs),
            [
                pltpu.VMEM((members * tokens, slots * tile), bf16),
                pltpu.VMEM((members * tokens, width), bf16),
                pltpu.VMEM((width, slots * tile), f32),
            ] + ([powers] if pieces else []),
        )

    def give_back(chunks):
        count = len(chunks)
        operands = [me, share, row_blocks, *grads]
        for j in chunks:
            operands += [*parts[j], shares[j], others[j]]
        products = call(
            functools.partial(grad_kernel, dims, chunks),
            operands, [SMEM] * 3 + [VMEM] * (len(operands) - 3),
            [pltpu.VMEM((tokens, count * 2 * quarter), bf16)] * members + [pltpu.VMEM((tokens, count * width), bf16)] * near,
            [VMEM] * (members + near),
            [pltpu.VMEM((3, 2 * quarter, depth), bf16), pltpu.VMEM((tokens, depth), bf16)],
        )
        arrived = {p: inside(products[p], p) for p in partners}
        olds = [products[0]] + [arrived[p] for p in range(1, members)]
        news = [products[members]] + [inside(products[members + q], q) for q in range(1, near)]
        return olds + news

    def join(base, base_tiles, first, added):
        return call(
            functools.partial(join_kernel, tile, half, first, base_tiles), (base, added), [VMEM, VMEM],
            coded(half), VMEM, [powers],
        )

    halves = range(2)
    sums_0, sums_1, (sums_2,), (own,) = partial(0, 2), partial(1, 2), partial(2, 1), partial(3, 0)
    i1 = [across(sums_0[n], inward) for n in halves]
    i2 = [across(sums_1[n], inward) for n in halves]
    i3 = across(sums_2, inward)
    x1 = [across(join(sums_1[n], half, 0, i1[n]), middle) for n in halves]
    x2 = [across(join(sums_2, tiles, n * half, i2[n]), middle) for n in halves]
    last = [across(join(sums_0[n], half, 0, x1[n]), outward) for n in halves]

    sets = {"a": (2,), "b": (1, 3), "c": (0,)}
    back = {name: give_back(chunks) for name, chunks in sets.items()}

    grad_tiles = call(
        functools.partial(finish_kernel, dims), (me, tile_mask, own, *last, i3, *x2),
        [SMEM, SMEM] + [VMEM] * 6, jax.ShapeDtypeStruct((cols, slots, tile, tile), f32), HBM,
        [pltpu.VMEM((cols, slots, tile, tile), f32), DMA((cols,))],
    )

    def unpack(chunks, pieces, extra):
        return call(
            functools.partial(unpack_kernel, dims, chunks, len(extra)),
            (me, *pieces, *extra), [SMEM] + [VMEM] * len(pieces) + [HBM] * len(extra),
            jax.ShapeDtypeStruct(hidden.shape, bf16), HBM, [DMA((2 * members * len(chunks),))],
            input_output_aliases={1 + len(pieces): 0} if extra else {},
        )

    result = []
    for name, chunks in sets.items():
        result = [unpack(chunks, back[name], result)]
    return result[0], grad_tiles


def solution(mesh):
    return jax.shard_map(
        on_device,
        mesh=mesh,
        in_specs=(
            P(("groups", "seqt"), None),
            P(("groups", "seqt"), None),
            P("seqt", None, None, None),
            P(),
            P("seqt", None),
        ),
        out_specs=(P(("groups", "seqt"), None), P(("groups", "seqt"), None, None, None)),
        check_vma=False,
    )
```

```python
import functools

import jax
import jax.numpy as jnp
from jax import lax
from jax.experimental import pallas as pl
from jax.experimental.pallas import tpu as pltpu
from jax.sharding import PartitionSpec as P


PLANES = 4
TOP = 32000.0
LIMIT = 8 * 1024 * 1024
HBM = pl.BlockSpec(memory_space=pltpu.HBM)
SMEM = pl.BlockSpec(memory_space=pltpu.SMEM)
VMEM = pl.BlockSpec(memory_space=pltpu.VMEM)
DMA = pltpu.SemaphoreType.DMA


def start_all(copies, sems):
    started = []
    for n, (src, dst) in enumerate(copies):
        copy = pltpu.make_async_copy(src, dst, sems.at[n])
        copy.start()
        started.append(copy)
    return started


def wait_all(started):
    for copy in started:
        copy.wait()


def plane_of(j, z):
    even = z % 2 == 0
    if j == 0:
        return jnp.where(even, 3, 0)
    if j == 1:
        return jnp.where(z < 2, z + 2, z - 2)
    if j == 2:
        return jnp.where(even, 1, 2)
    return z


def owner(j, p, members, me_ref):
    z, m = me_ref[0] // members, me_ref[0] % members
    return plane_of(j, z) * members + (m ^ p)


def block(index, size):
    return pl.ds(pl.multiple_of(index * size, 128), size)


def pack_kernel(dims, chunks, me_ref, rows_ref, grad_ref, hidden_ref, *refs):
    members, _, cols, slots, tile = dims
    outs, sems = refs[:-1], refs[-1]
    width = cols * tile
    copies = []
    for n, j in enumerate(chunks):
        for p in range(members):
            out, who = outs[n * members + p], owner(j, p, members, me_ref)
            copies.append((hidden_ref.at[:, block(who, width)], out.at[:, pl.ds(0, width)]))
            for k in range(slots):
                copies.append((grad_ref.at[:, block(rows_ref[k, who], tile)], out.at[:, pl.ds(width + k * tile, tile)]))
    wait_all(start_all(copies, sems))


def mask_kernel(cols, slots, tile, share_ref, mask_ref, tiles_ref, own, crossing, matrix):
    for c in range(cols):
        for k in range(slots):
            factor = mask_ref[k, c].astype(jnp.float32).astype(jnp.bfloat16)
            matrix[pl.ds(c * tile, tile), pl.ds(k * tile, tile)] = tiles_ref[c, k] * factor
    quarter = cols * tile // 4
    own[pl.ds(0, quarter), :] = matrix[pl.ds(pl.multiple_of(share_ref[0] * quarter, 16), quarter), :]
    new = matrix[pl.ds(pl.multiple_of((2 + share_ref[0]) * quarter, 16), quarter), :]
    own[pl.ds(quarter, quarter), :] = new
    crossing[...] = new


def bundle_kernel(own, crossed, out):
    rows = own.shape[0]
    out[pl.ds(0, rows), :] = own[...]
    out[pl.ds(rows, crossed.shape[0]), :] = crossed[...]


def pick_kernel(members, me_ref, at_end, inside, out):
    outer = (me_ref[0] < members) | (me_ref[0] >= 3 * members)

    @pl.when(outer)
    def _():
        out[...] = at_end[...]

    @pl.when(jnp.logical_not(outer))
    def _():
        out[...] = inside[...]


def decode(ref, tiles, tile, n):
    scale = jnp.exp2(ref[pl.ds(tiles * tile + n, 1), :].astype(jnp.float32)) * (1.0 / TOP)
    return ref[pl.ds(n * tile, tile), :].astype(jnp.float32) * scale


def encode(value, out, powers, tile, n):
    top = jnp.max(jnp.abs(value), axis=0, keepdims=True)
    power = jnp.ceil(jnp.log2(jnp.maximum(top, 1e-30)))
    code = jnp.round(value * (jnp.exp2(-power) * TOP))
    out[pl.ds(n * tile, tile), :] = code.astype(jnp.int32).astype(jnp.int16)
    powers[pl.ds(n, 1), :] = power


def flush_powers(out, powers, first):
    rows = out.shape[0] - first
    out[pl.ds(first, rows), :] = powers[pl.ds(0, rows), :].astype(jnp.int32).astype(jnp.int16)


def partial_kernel(dims, counts, *refs):
    members, tokens, cols, slots, tile = dims
    tiles, width = cols * slots, cols * tile
    parts, refs = refs[:members], refs[members:]
    messages = max(len(counts), 1)
    outs, (picks, held, total, *powers) = refs[:messages], refs[messages:]
    for p, part in enumerate(parts):
        rows = pl.ds(p * tokens, tokens)
        held[rows, :] = part[:, pl.ds(0, width)]
        picks[rows, :] = part[:, pl.ds(width, slots * tile)]
    total[...] = lax.dot_general(held[...], picks[...], (((0,), (0,)), ((), ())), preferred_element_type=jnp.float32)
    if counts:
        n = 0
        for out, count in zip(outs, counts):
            for i in range(count):
                c, k = divmod(n, slots)
                encode(total[pl.ds(c * tile, tile), pl.ds(k * tile, tile)], out, powers[0], tile, i)
                n += 1
            flush_powers(out, powers[0], count * tile)
    else:
        for n in range(tiles):
            c, k = divmod(n, slots)
            outs[0][pl.ds(n * tile, tile), :] = total[pl.ds(c * tile, tile), pl.ds(k * tile, tile)]


def join_kernel(tile, tiles, first, base_tiles, base, added, out, powers):
    for n in range(tiles):
        encode(decode(base, base_tiles, tile, first + n) + decode(added, tiles, tile, n), out, powers, tile, n)
    flush_powers(out, powers, tiles * tile)


def finish_kernel(dims, split, me_ref, mask_ref, own, out_a, out_b, inward, mid_a, mid_b, out, made, sems):
    members, _, cols, slots, tile = dims
    tiles = cols * slots

    def run(first, second, wholes):
        writes = []
        for c in range(cols):
            for k in range(slots):
                n = c * slots + k
                value = own[pl.ds(n * tile, tile), :] + (
                    decode(first, split, tile, n) if n < split else decode(second, tiles - split, tile, n - split)
                )
                for source in wholes:
                    value = value + decode(source, tiles, tile, n)
                made[c, k] = value * mask_ref[k, c].astype(jnp.float32)
            write = pltpu.make_async_copy(made.at[c], out.at[c], sems.at[c])
            write.start()
            writes.append(write)
        wait_all(writes)

    outer = (me_ref[0] < members) | (me_ref[0] >= 3 * members)
    pl.when(outer)(lambda: run(out_a, out_b, ()))
    pl.when(jnp.logical_not(outer))(lambda: run(mid_a, mid_b, (inward,)))


def grad_kernel(dims, chunks, me_ref, share_ref, rows_ref, *refs):
    members, _, cols, slots, tile = dims
    width, near = cols * tile, members // 2
    quarter = width // 4
    refs = list(refs)
    grads = [refs.pop(0) for _ in range(near)]
    inputs = [([refs.pop(0) for _ in range(members)], refs.pop(0), refs.pop(0)) for _ in chunks]
    olds, news, (weights, picks) = refs[:members], refs[members:members + near], refs[members + near:]

    def product(rows, n):
        made = lax.dot_general(rows, weights[n], (((1,), (1,)), ((), ())), preferred_element_type=jnp.float32)
        return made.astype(jnp.bfloat16)

    for n, j in enumerate(chunks):
        parts, mine, other = inputs[n]
        for i in range(3):
            rows = pl.ds(i * quarter, quarter)
            weights[i, pl.ds(pl.multiple_of(share_ref[0] * quarter, 16), quarter), :] = mine[rows, :]
            weights[i, pl.ds(pl.multiple_of((1 - share_ref[0]) * quarter, 16), quarter), :] = other[rows, :]
        picked = pl.ds(width, slots * tile)
        for p in range(members):
            olds[p][:, pl.ds(n * 2 * quarter, 2 * quarter)] = product(parts[p][:, picked], 0)
        across = owner(j, near, members, me_ref)
        for q in range(near):
            for k in range(slots):
                picks[:, pl.ds(k * tile, tile)] = grads[q][:, block(rows_ref[k, across], tile)]
            news[q][:, pl.ds(n * width, 2 * quarter)] = product(parts[q][:, picked], 1)
            news[q][:, pl.ds(n * width + 2 * quarter, 2 * quarter)] = product(picks[...], 2)


def unpack_kernel(dims, chunks, aliased, me_ref, *refs):
    members, _, cols, _, tile = dims
    width, near = cols * tile, members // 2
    half = width // 2
    count = members + near
    olds, news, out, sems = refs[:members], refs[members:count], refs[count + aliased], refs[-1]
    copies = []
    for n, j in enumerate(chunks):
        for p in range(members):
            who = owner(j, p, members, me_ref)
            copies.append((olds[p].at[:, pl.ds(n * half, half)], out.at[:, pl.ds(pl.multiple_of(who * width, 128), half)]))
            piece = news[p % near].at[:, pl.ds(n * width + (p // near) * half, half)]
            copies.append((piece, out.at[:, pl.ds(pl.multiple_of(who * width + half, 128), half)]))
    wait_all(start_all(copies, sems))


def on_device(out_grad, hidden, down_tiles, row_blocks, tile_mask):
    devices = lax.axis_size("seqt")
    members = devices // PLANES
    tokens = out_grad.shape[0]
    cols, slots, tile = down_tiles.shape[:3]
    width, tiles = cols * tile, cols * slots
    dims = (members, tokens, cols, slots, tile)
    scale_rows = -(-tiles // 16) * 16
    me = jnp.full((1,), lax.axis_index("seqt"), jnp.int32)
    row_blocks, tile_mask = row_blocks.T, tile_mask.T
    rows_early, mask_early = [pltpu.with_memory_space_constraint(value, pltpu.HBM) for value in (row_blocks, tile_mask)]
    share = jnp.full((1,), lax.axis_index("groups") & 1, jnp.int32)
    near = members // 2
    own_grad = pltpu.with_memory_space_constraint(out_grad, pltpu.VMEM)
    out_grad, hidden = [pltpu.with_memory_space_constraint(value, pltpu.HBM) for value in (out_grad, hidden)]
    bf16, f32 = jnp.bfloat16, jnp.float32
    half = members // 2
    partners = sorted(range(1, members), key=lambda p: (p < half, p))

    def call(kernel, operands, specs, outs, out_specs, scratch, **extra):
        return pl.pallas_call(
            kernel, out_shape=outs, in_specs=specs, out_specs=out_specs, scratch_shapes=scratch,
            compiler_params=pltpu.CompilerParams(vmem_limit_bytes=LIMIT), **extra,
        )(*operands)

    def permute(value, pairs):
        return pltpu.with_memory_space_constraint(lax.ppermute(value, "seqt", pairs), pltpu.VMEM)

    def inside(value, p):
        return permute(value, [(i, i ^ p) for i in range(devices)])

    def over_x(value):
        moved = lax.ppermute(value, "groups", [(i, i ^ 1) for i in range(lax.axis_size("groups"))])
        return pltpu.with_memory_space_constraint(moved, pltpu.VMEM)

    def across(value, pairs):
        return permute(value, [(a * members + i, b * members + i) for a, b in pairs for i in range(members)])

    parts = [None] * PLANES
    for chunks in ((0,), (1, 2, 3)):
        count = len(chunks) * members
        packed = call(
            functools.partial(pack_kernel, dims, chunks),
            (me, rows_early, out_grad, hidden), [SMEM, SMEM, HBM, HBM],
            [pltpu.VMEM((tokens, width + slots * tile), bf16)] * count,
            [VMEM] * count, [DMA((count * (slots + 1),))],
        )
        for n, j in enumerate(chunks):
            mine = packed[n * members:(n + 1) * members]
            arrived = {p: inside(mine[p], p) for p in partners}
            parts[j] = [mine[0]] + [arrived[p] for p in range(1, members)]

    grads = [own_grad] + [inside(out_grad, q) for q in range(1, near)]

    depth, quarter = slots * tile, width // 4
    own_rows, crossing = call(
        functools.partial(mask_kernel, cols, slots, tile), (share, mask_early, down_tiles), [SMEM, SMEM, VMEM],
        [pltpu.VMEM((2 * quarter, depth), bf16), pltpu.VMEM((quarter, depth), bf16)], [VMEM, VMEM],
        [pltpu.VMEM((width, depth), bf16)],
    )
    bundle = call(
        bundle_kernel, (own_rows, inside(crossing, near)), [VMEM, VMEM],
        pltpu.VMEM((3 * quarter, depth), bf16), VMEM, [],
    )
    pairs, inward, middle, outward = [(0, 1), (1, 0), (2, 3), (3, 2)], [(0, 1), (3, 2)], [(1, 2), (2, 1)], [(1, 0), (2, 3)]
    e1, m1 = across(bundle, pairs), across(bundle, middle)
    m2, o1 = across(e1, middle), across(m1, outward)
    o2 = across(m2, outward)

    def pick(at_end, inner):
        return call(
            functools.partial(pick_kernel, members), (me, at_end, inner), [SMEM, VMEM, VMEM],
            pltpu.VMEM((3 * quarter, depth), bf16), VMEM, [],
        )

    shares = {3: bundle, 2: pick(e1, m1), 1: pick(o1, m2), 0: pick(o2, e1)}
    others = {j: over_x(value) for j, value in shares.items()}

    def coded(count):
        return pltpu.VMEM((count * tile + -(-count // 16) * 16, tile), jnp.int16)

    powers = pltpu.VMEM((scale_rows, tile), f32)

    def partial(j, counts):
        outs = [coded(count) for count in counts] or [pltpu.VMEM((tiles * tile, tile), f32)]
        return call(
            functools.partial(partial_kernel, dims, counts), parts[j], [VMEM] * members,
            outs, [VMEM] * len(outs),
            [
                pltpu.VMEM((members * tokens, slots * tile), bf16),
                pltpu.VMEM((members * tokens, width), bf16),
                pltpu.VMEM((width, slots * tile), f32),
            ] + ([powers] if counts else []),
        )

    def give_back(chunks):
        count = len(chunks)
        operands = [me, share, row_blocks, *grads]
        for j in chunks:
            operands += [*parts[j], shares[j], others[j]]
        products = call(
            functools.partial(grad_kernel, dims, chunks),
            operands, [SMEM] * 3 + [VMEM] * (len(operands) - 3),
            [pltpu.VMEM((tokens, count * 2 * quarter), bf16)] * members + [pltpu.VMEM((tokens, count * width), bf16)] * near,
            [VMEM] * (members + near),
            [pltpu.VMEM((3, 2 * quarter, depth), bf16), pltpu.VMEM((tokens, depth), bf16)],
        )
        arrived = {p: inside(products[p], p) for p in partners}
        olds = [products[0]] + [arrived[p] for p in range(1, members)]
        news = [products[members]] + [inside(products[members + q], q) for q in range(1, near)]
        return olds + news

    def join(count, base, base_tiles, first, added):
        return call(
            functools.partial(join_kernel, tile, count, first, base_tiles), (base, added), [VMEM, VMEM],
            coded(count), VMEM, [powers],
        )

    counts = (tiles * 5 // 8, tiles - tiles * 5 // 8)
    firsts = (0, counts[0])
    sums_0, sums_1, (sums_2,), (own,) = partial(0, counts), partial(1, counts), partial(2, (tiles,)), partial(3, ())
    i1 = [across(sums_0[n], inward) for n in range(2)]
    i2 = [across(sums_1[n], inward) for n in range(2)]
    i3 = across(sums_2, inward)
    x1, x2, last = [], [], []
    for n, (count, first) in enumerate(zip(counts, firsts)):
        x1.append(across(join(count, sums_1[n], count, 0, i1[n]), middle))
        x2.append(across(join(count, sums_2, tiles, first, i2[n]), middle))
        last.append(across(join(count, sums_0[n], count, 0, x1[n]), outward))

    sets = {"a": (2,), "b": (1, 3), "c": (0,)}
    back = {name: give_back(chunks) for name, chunks in sets.items()}

    grad_tiles = call(
        functools.partial(finish_kernel, dims, counts[0]), (me, tile_mask, own, *last, i3, *x2),
        [SMEM, SMEM] + [VMEM] * 6, jax.ShapeDtypeStruct((cols, slots, tile, tile), f32), HBM,
        [pltpu.VMEM((cols, slots, tile, tile), f32), DMA((cols,))],
    )

    def unpack(chunks, pieces, extra):
        return call(
            functools.partial(unpack_kernel, dims, chunks, len(extra)),
            (me, *pieces, *extra), [SMEM] + [VMEM] * len(pieces) + [HBM] * len(extra),
            jax.ShapeDtypeStruct(hidden.shape, bf16), HBM, [DMA((2 * members * len(chunks),))],
            input_output_aliases={1 + len(pieces): 0} if extra else {},
        )

    result = []
    for name, chunks in sets.items():
        result = [unpack(chunks, back[name], result)]
    return result[0], grad_tiles


def solution(mesh):
    return jax.shard_map(
        on_device,
        mesh=mesh,
        in_specs=(
            P(("groups", "seqt"), None),
            P(("groups", "seqt"), None),
            P("seqt", None, None, None),
            P(),
            P("seqt", None),
        ),
        out_specs=(P(("groups", "seqt"), None), P(("groups", "seqt"), None, None, None)),
        check_vma=False,
    )
```

```python
import functools

import jax
import jax.numpy as jnp
from jax import lax
from jax.experimental import pallas as pl
from jax.experimental.pallas import tpu as pltpu
from jax.sharding import PartitionSpec as P


PLANES = 4
TOP = 32000.0
LIMIT = 8 * 1024 * 1024
HBM = pl.BlockSpec(memory_space=pltpu.HBM)
SMEM = pl.BlockSpec(memory_space=pltpu.SMEM)
VMEM = pl.BlockSpec(memory_space=pltpu.VMEM)
DMA = pltpu.SemaphoreType.DMA


def start_all(copies, sems):
    started = []
    for n, (src, dst) in enumerate(copies):
        copy = pltpu.make_async_copy(src, dst, sems.at[n])
        copy.start()
        started.append(copy)
    return started


def wait_all(started):
    for copy in started:
        copy.wait()


def plane_of(j, z):
    even = z % 2 == 0
    if j == 0:
        return jnp.where(even, 3, 0)
    if j == 1:
        return jnp.where(z < 2, z + 2, z - 2)
    if j == 2:
        return jnp.where(even, 1, 2)
    return z


def owner(j, p, members, me_ref):
    z, m = me_ref[0] // members, me_ref[0] % members
    return plane_of(j, z) * members + (m ^ p)


def block(index, size):
    return pl.ds(pl.multiple_of(index * size, 128), size)


def pack_kernel(dims, chunks, me_ref, rows_ref, grad_ref, hidden_ref, *refs):
    members, _, cols, slots, tile = dims
    outs, sems = refs[:-1], refs[-1]
    width = cols * tile
    copies = []
    for n, j in enumerate(chunks):
        for p in range(members):
            out, who = outs[n * members + p], owner(j, p, members, me_ref)
            copies.append((hidden_ref.at[:, block(who, width)], out.at[:, pl.ds(0, width)]))
            for k in range(slots):
                copies.append((grad_ref.at[:, block(rows_ref[k, who], tile)], out.at[:, pl.ds(width + k * tile, tile)]))
    wait_all(start_all(copies, sems))


def cross_kernel(cols, slots, tile, share_ref, mask_ref, tiles_ref, crossing, loaded, sems):
    quarter = cols * tile // 4
    rows = min(quarter, tile)
    start = (2 + share_ref[0]) * quarter
    inner = pl.multiple_of(start % tile, 16)
    columns = [start // tile + n for n in range(quarter // rows)]
    wait_all(start_all([(tiles_ref.at[c, :, pl.ds(inner, rows), :], loaded.at[n]) for n, c in enumerate(columns)], sems))
    for n, c in enumerate(columns):
        for k in range(slots):
            factor = mask_ref[k, c].astype(jnp.float32).astype(jnp.bfloat16)
            crossing[pl.ds(n * rows, rows), pl.ds(k * tile, tile)] = loaded[n, k] * factor


def mask_kernel(cols, slots, tile, share_ref, mask_ref, tiles_ref, crossing, own, matrix):
    for c in range(cols // 2):
        for k in range(slots):
            factor = mask_ref[k, c].astype(jnp.float32).astype(jnp.bfloat16)
            matrix[pl.ds(c * tile, tile), pl.ds(k * tile, tile)] = tiles_ref[c, k] * factor
    quarter = cols * tile // 4
    own[pl.ds(0, quarter), :] = matrix[pl.ds(pl.multiple_of(share_ref[0] * quarter, 16), quarter), :]
    own[pl.ds(quarter, quarter), :] = crossing[...]


def bundle_kernel(own, crossed, out):
    rows = own.shape[0]
    out[pl.ds(0, rows), :] = own[...]
    out[pl.ds(rows, crossed.shape[0]), :] = crossed[...]


def pick_kernel(members, me_ref, at_end, inside, out):
    outer = (me_ref[0] < members) | (me_ref[0] >= 3 * members)

    @pl.when(outer)
    def _():
        out[...] = at_end[...]

    @pl.when(jnp.logical_not(outer))
    def _():
        out[...] = inside[...]


def decode(ref, tiles, tile, n):
    scale = jnp.exp2(ref[pl.ds(tiles * tile + n, 1), :].astype(jnp.float32)) * (1.0 / TOP)
    return ref[pl.ds(n * tile, tile), :].astype(jnp.float32) * scale


def encode(value, out, powers, tile, n):
    top = jnp.max(jnp.abs(value), axis=0, keepdims=True)
    power = jnp.ceil(jnp.log2(jnp.maximum(top, 1e-30)))
    code = jnp.round(value * (jnp.exp2(-power) * TOP))
    out[pl.ds(n * tile, tile), :] = code.astype(jnp.int32).astype(jnp.int16)
    powers[pl.ds(n, 1), :] = power


def flush_powers(out, powers, first):
    rows = out.shape[0] - first
    out[pl.ds(first, rows), :] = powers[pl.ds(0, rows), :].astype(jnp.int32).astype(jnp.int16)


def partial_kernel(dims, counts, *refs):
    members, tokens, cols, slots, tile = dims
    tiles, width = cols * slots, cols * tile
    parts, refs = refs[:members], refs[members:]
    messages = max(len(counts), 1)
    outs, (picks, held, total, *powers) = refs[:messages], refs[messages:]
    for p, part in enumerate(parts):
        rows = pl.ds(p * tokens, tokens)
        held[rows, :] = part[:, pl.ds(0, width)]
        picks[rows, :] = part[:, pl.ds(width, slots * tile)]
    total[...] = lax.dot_general(held[...], picks[...], (((0,), (0,)), ((), ())), preferred_element_type=jnp.float32)
    if counts:
        n = 0
        for out, count in zip(outs, counts):
            for i in range(count):
                c, k = divmod(n, slots)
                encode(total[pl.ds(c * tile, tile), pl.ds(k * tile, tile)], out, powers[0], tile, i)
                n += 1
            flush_powers(out, powers[0], count * tile)
    else:
        for n in range(tiles):
            c, k = divmod(n, slots)
            outs[0][pl.ds(n * tile, tile), :] = total[pl.ds(c * tile, tile), pl.ds(k * tile, tile)]


def join_kernel(tile, tiles, base, added, out, powers):
    for n in range(tiles):
        encode(decode(base, tiles, tile, n) + decode(added, tiles, tile, n), out, powers, tile, n)
    flush_powers(out, powers, tiles * tile)


def finish_kernel(dims, first, count, me_ref, mask_ref, own, outward, inward, middle, *refs):
    members, _, _, slots, tile = dims
    out, made, sems = refs[-3:]
    places = [divmod(first + i, slots) for i in range(count)]
    writes = [pltpu.make_async_copy(made.at[i], out.at[c, k], sems.at[i]) for i, (c, k) in enumerate(places)]

    def run(sources):
        for i, (c, k) in enumerate(places):
            value = own[pl.ds((first + i) * tile, tile), :]
            for source in sources:
                value = value + decode(source, count, tile, i)
            made[i] = value * mask_ref[k, c].astype(jnp.float32)
            writes[i].start()

    outer = (me_ref[0] < members) | (me_ref[0] >= 3 * members)
    pl.when(outer)(lambda: run((outward,)))
    pl.when(jnp.logical_not(outer))(lambda: run((inward, middle)))
    wait_all(writes)


def grad_kernel(dims, chunks, me_ref, share_ref, rows_ref, *refs):
    members, _, cols, slots, tile = dims
    width, near = cols * tile, members // 2
    quarter = width // 4
    refs = list(refs)
    grads = [refs.pop(0) for _ in range(near)]
    inputs = [([refs.pop(0) for _ in range(members)], refs.pop(0), refs.pop(0)) for _ in chunks]
    olds, news, (weights, picks) = refs[:members], refs[members:members + near], refs[members + near:]

    def product(rows, n):
        made = lax.dot_general(rows, weights[n], (((1,), (1,)), ((), ())), preferred_element_type=jnp.float32)
        return made.astype(jnp.bfloat16)

    for n, j in enumerate(chunks):
        parts, mine, other = inputs[n]
        for i in range(3):
            rows = pl.ds(i * quarter, quarter)
            weights[i, pl.ds(pl.multiple_of(share_ref[0] * quarter, 16), quarter), :] = mine[rows, :]
            weights[i, pl.ds(pl.multiple_of((1 - share_ref[0]) * quarter, 16), quarter), :] = other[rows, :]
        picked = pl.ds(width, slots * tile)
        for p in range(members):
            olds[p][:, pl.ds(n * 2 * quarter, 2 * quarter)] = product(parts[p][:, picked], 0)
        across = owner(j, near, members, me_ref)
        for q in range(near):
            for k in range(slots):
                picks[:, pl.ds(k * tile, tile)] = grads[q][:, block(rows_ref[k, across], tile)]
            news[q][:, pl.ds(n * width, 2 * quarter)] = product(parts[q][:, picked], 1)
            news[q][:, pl.ds(n * width + 2 * quarter, 2 * quarter)] = product(picks[...], 2)


def unpack_kernel(dims, chunks, aliased, me_ref, *refs):
    members, _, cols, _, tile = dims
    width, near = cols * tile, members // 2
    half = width // 2
    count = members + near
    olds, news, out, sems = refs[:members], refs[members:count], refs[count + aliased], refs[-1]
    copies = []
    for n, j in enumerate(chunks):
        for p in range(members):
            who = owner(j, p, members, me_ref)
            copies.append((olds[p].at[:, pl.ds(n * half, half)], out.at[:, pl.ds(pl.multiple_of(who * width, 128), half)]))
            piece = news[p % near].at[:, pl.ds(n * width + (p // near) * half, half)]
            copies.append((piece, out.at[:, pl.ds(pl.multiple_of(who * width + half, 128), half)]))
    wait_all(start_all(copies, sems))


def on_device(out_grad, hidden, down_tiles, row_blocks, tile_mask):
    devices = lax.axis_size("seqt")
    members = devices // PLANES
    tokens = out_grad.shape[0]
    cols, slots, tile = down_tiles.shape[:3]
    width, tiles = cols * tile, cols * slots
    dims = (members, tokens, cols, slots, tile)
    scale_rows = -(-tiles // 16) * 16
    me = jnp.full((1,), lax.axis_index("seqt"), jnp.int32)
    row_blocks, tile_mask = row_blocks.T, tile_mask.T
    rows_early, mask_early = [pltpu.with_memory_space_constraint(value, pltpu.HBM) for value in (row_blocks, tile_mask)]
    share = jnp.full((1,), lax.axis_index("groups") & 1, jnp.int32)
    near = members // 2
    own_grad = pltpu.with_memory_space_constraint(out_grad, pltpu.VMEM)
    out_grad, hidden = [pltpu.with_memory_space_constraint(value, pltpu.HBM) for value in (out_grad, hidden)]
    bf16, f32 = jnp.bfloat16, jnp.float32
    half = members // 2
    partners = sorted(range(1, members), key=lambda p: (p < half, p))

    def call(kernel, operands, specs, outs, out_specs, scratch, **extra):
        return pl.pallas_call(
            kernel, out_shape=outs, in_specs=specs, out_specs=out_specs, scratch_shapes=scratch,
            compiler_params=pltpu.CompilerParams(vmem_limit_bytes=LIMIT), **extra,
        )(*operands)

    def permute(value, pairs):
        return pltpu.with_memory_space_constraint(lax.ppermute(value, "seqt", pairs), pltpu.VMEM)

    def inside(value, p):
        return permute(value, [(i, i ^ p) for i in range(devices)])

    def over_x(value):
        moved = lax.ppermute(value, "groups", [(i, i ^ 1) for i in range(lax.axis_size("groups"))])
        return pltpu.with_memory_space_constraint(moved, pltpu.VMEM)

    def across(value, pairs):
        return permute(value, [(a * members + i, b * members + i) for a, b in pairs for i in range(members)])

    parts = [None] * PLANES
    for chunks in ((0,), (1, 2, 3)):
        count = len(chunks) * members
        packed = call(
            functools.partial(pack_kernel, dims, chunks),
            (me, rows_early, out_grad, hidden), [SMEM, SMEM, HBM, HBM],
            [pltpu.VMEM((tokens, width + slots * tile), bf16)] * count,
            [VMEM] * count, [DMA((count * (slots + 1),))],
        )
        for n, j in enumerate(chunks):
            mine = packed[n * members:(n + 1) * members]
            arrived = {p: inside(mine[p], p) for p in partners}
            parts[j] = [mine[0]] + [arrived[p] for p in range(1, members)]

    grads = [own_grad] + [inside(out_grad, q) for q in range(1, near)]

    depth, quarter = slots * tile, width // 4
    rows = min(quarter, tile)
    crossing = call(
        functools.partial(cross_kernel, cols, slots, tile),
        (share, mask_early, pltpu.with_memory_space_constraint(down_tiles, pltpu.HBM)), [SMEM, SMEM, HBM],
        pltpu.VMEM((quarter, depth), bf16), VMEM,
        [pltpu.VMEM((quarter // rows, slots, rows, tile), bf16), DMA((quarter // rows,))],
    )
    own_rows = call(
        functools.partial(mask_kernel, cols, slots, tile), (share, mask_early, down_tiles, crossing),
        [SMEM, SMEM, VMEM, VMEM], pltpu.VMEM((2 * quarter, depth), bf16), VMEM,
        [pltpu.VMEM((2 * quarter, depth), bf16)],
    )
    bundle = call(
        bundle_kernel, (own_rows, inside(crossing, near)), [VMEM, VMEM],
        pltpu.VMEM((3 * quarter, depth), bf16), VMEM, [],
    )
    pairs, inward, middle, outward = [(0, 1), (1, 0), (2, 3), (3, 2)], [(0, 1), (3, 2)], [(1, 2), (2, 1)], [(1, 0), (2, 3)]
    e1, m1 = across(bundle, pairs), across(bundle, middle)
    m2, o1 = across(e1, middle), across(m1, outward)
    o2 = across(m2, outward)

    def pick(at_end, inner):
        return call(
            functools.partial(pick_kernel, members), (me, at_end, inner), [SMEM, VMEM, VMEM],
            pltpu.VMEM((3 * quarter, depth), bf16), VMEM, [],
        )

    shares = {3: bundle, 2: pick(e1, m1), 1: pick(o1, m2), 0: pick(o2, e1)}
    others = {j: over_x(value) for j, value in shares.items()}

    def coded(count):
        return pltpu.VMEM((count * tile + -(-count // 16) * 16, tile), jnp.int16)

    powers = pltpu.VMEM((scale_rows, tile), f32)

    def partial(j, counts):
        outs = [coded(count) for count in counts] or [pltpu.VMEM((tiles * tile, tile), f32)]
        return call(
            functools.partial(partial_kernel, dims, counts), parts[j], [VMEM] * members,
            outs, [VMEM] * len(outs),
            [
                pltpu.VMEM((members * tokens, slots * tile), bf16),
                pltpu.VMEM((members * tokens, width), bf16),
                pltpu.VMEM((width, slots * tile), f32),
            ] + ([powers] if counts else []),
        )

    def give_back(chunks):
        count = len(chunks)
        operands = [me, share, row_blocks, *grads]
        for j in chunks:
            operands += [*parts[j], shares[j], others[j]]
        products = call(
            functools.partial(grad_kernel, dims, chunks),
            operands, [SMEM] * 3 + [VMEM] * (len(operands) - 3),
            [pltpu.VMEM((tokens, count * 2 * quarter), bf16)] * members + [pltpu.VMEM((tokens, count * width), bf16)] * near,
            [VMEM] * (members + near),
            [pltpu.VMEM((3, 2 * quarter, depth), bf16), pltpu.VMEM((tokens, depth), bf16)],
        )
        arrived = {p: inside(products[p], p) for p in partners}
        olds = [products[0]] + [arrived[p] for p in range(1, members)]
        news = [products[members]] + [inside(products[members + q], q) for q in range(1, near)]
        return olds + news

    def join(count, base, added):
        return call(
            functools.partial(join_kernel, tile, count), (base, added), [VMEM, VMEM],
            coded(count), VMEM, [powers],
        )

    counts = (tiles * 5 // 8, tiles - tiles * 5 // 8)
    firsts = (0, counts[0])
    sums_0, sums_1, sums_2, (own,) = partial(0, counts), partial(1, counts), partial(2, counts), partial(3, ())
    i1 = [across(sums_0[n], inward) for n in range(2)]
    i2 = [across(sums_1[n], inward) for n in range(2)]
    i3 = [across(sums_2[n], inward) for n in range(2)]
    x1, x2, last = [], [], []
    for n, count in enumerate(counts):
        x1.append(across(join(count, sums_1[n], i1[n]), middle))
        x2.append(across(join(count, sums_2[n], i2[n]), middle))
        last.append(across(join(count, sums_0[n], x1[n]), outward))

    sets = {"a": (2,), "b": (1, 3), "c": (0,)}
    back = {name: give_back(chunks) for name, chunks in sets.items()}

    grad_tiles = []
    for n, (count, first) in enumerate(zip(counts, firsts)):
        grad_tiles = [call(
            functools.partial(finish_kernel, dims, first, count),
            (me, tile_mask, own, last[n], i3[n], x2[n], *grad_tiles), [SMEM, SMEM] + [VMEM] * 4 + [HBM] * n,
            jax.ShapeDtypeStruct((cols, slots, tile, tile), f32), HBM,
            [pltpu.VMEM((count, tile, tile), f32), DMA((count,))],
            input_output_aliases={6: 0} if n else {},
        )]

    def unpack(chunks, pieces, extra):
        return call(
            functools.partial(unpack_kernel, dims, chunks, len(extra)),
            (me, *pieces, *extra), [SMEM] + [VMEM] * len(pieces) + [HBM] * len(extra),
            jax.ShapeDtypeStruct(hidden.shape, bf16), HBM, [DMA((2 * members * len(chunks),))],
            input_output_aliases={1 + len(pieces): 0} if extra else {},
        )

    result = []
    for name, chunks in sets.items():
        result = [unpack(chunks, back[name], result)]
    return result[0], grad_tiles[0]


def solution(mesh):
    return jax.shard_map(
        on_device,
        mesh=mesh,
        in_specs=(
            P(("groups", "seqt"), None),
            P(("groups", "seqt"), None),
            P("seqt", None, None, None),
            P(),
            P("seqt", None),
        ),
        out_specs=(P(("groups", "seqt"), None), P(("groups", "seqt"), None, None, None)),
        check_vma=False,
    )
```

```python
import functools

import jax
import jax.numpy as jnp
from jax import lax
from jax.experimental import pallas as pl
from jax.experimental.pallas import tpu as pltpu
from jax.sharding import PartitionSpec as P


PLANES = 4
TOP = 32000.0
LIMIT = 8 * 1024 * 1024
HBM = pl.BlockSpec(memory_space=pltpu.HBM)
SMEM = pl.BlockSpec(memory_space=pltpu.SMEM)
VMEM = pl.BlockSpec(memory_space=pltpu.VMEM)
DMA = pltpu.SemaphoreType.DMA


def start_all(copies, sems):
    started = []
    for n, (src, dst) in enumerate(copies):
        copy = pltpu.make_async_copy(src, dst, sems.at[n])
        copy.start()
        started.append(copy)
    return started


def wait_all(started):
    for copy in started:
        copy.wait()


def plane_of(j, z):
    even = z % 2 == 0
    if j == 0:
        return jnp.where(even, 3, 0)
    if j == 1:
        return jnp.where(z < 2, z + 2, z - 2)
    if j == 2:
        return jnp.where(even, 1, 2)
    return z


def owner(j, p, members, me_ref):
    z, m = me_ref[0] // members, me_ref[0] % members
    return plane_of(j, z) * members + (m ^ p)


def block(index, size):
    return pl.ds(pl.multiple_of(index * size, 128), size)


def pack_kernel(dims, chunks, me_ref, rows_ref, grad_ref, hidden_ref, *refs):
    members, _, cols, slots, tile = dims
    outs, sems = refs[:-1], refs[-1]
    width = cols * tile
    copies = []
    for n, j in enumerate(chunks):
        for p in range(members):
            out, who = outs[n * members + p], owner(j, p, members, me_ref)
            copies.append((hidden_ref.at[:, block(who, width)], out.at[:, pl.ds(0, width)]))
            for k in range(slots):
                copies.append((grad_ref.at[:, block(rows_ref[k, who], tile)], out.at[:, pl.ds(width + k * tile, tile)]))
    wait_all(start_all(copies, sems))


def cross_kernel(cols, slots, tile, share_ref, mask_ref, tiles_ref, crossing, loaded, sems):
    quarter = cols * tile // 4
    rows = min(quarter, tile)
    start = (2 + share_ref[0]) * quarter
    inner = pl.multiple_of(start % tile, 16)
    columns = [start // tile + n for n in range(quarter // rows)]
    wait_all(start_all([(tiles_ref.at[c, :, pl.ds(inner, rows), :], loaded.at[n]) for n, c in enumerate(columns)], sems))
    for n, c in enumerate(columns):
        for k in range(slots):
            factor = mask_ref[k, c].astype(jnp.float32).astype(jnp.bfloat16)
            crossing[pl.ds(n * rows, rows), pl.ds(k * tile, tile)] = loaded[n, k] * factor


def mask_kernel(cols, slots, tile, share_ref, mask_ref, tiles_ref, crossing, own, matrix):
    for c in range(cols // 2):
        for k in range(slots):
            factor = mask_ref[k, c].astype(jnp.float32).astype(jnp.bfloat16)
            matrix[pl.ds(c * tile, tile), pl.ds(k * tile, tile)] = tiles_ref[c, k] * factor
    quarter = cols * tile // 4
    own[pl.ds(0, quarter), :] = matrix[pl.ds(pl.multiple_of(share_ref[0] * quarter, 16), quarter), :]
    own[pl.ds(quarter, quarter), :] = crossing[...]


def bundle_kernel(own, crossed, out):
    rows = own.shape[0]
    out[pl.ds(0, rows), :] = own[...]
    out[pl.ds(rows, crossed.shape[0]), :] = crossed[...]


def pick_kernel(members, me_ref, at_end, inside, out):
    outer = (me_ref[0] < members) | (me_ref[0] >= 3 * members)

    @pl.when(outer)
    def _():
        out[...] = at_end[...]

    @pl.when(jnp.logical_not(outer))
    def _():
        out[...] = inside[...]


def decode(ref, tiles, tile, n):
    scale = jnp.exp2(ref[pl.ds(tiles * tile + n, 1), :].astype(jnp.float32)) * (1.0 / TOP)
    return ref[pl.ds(n * tile, tile), :].astype(jnp.float32) * scale


def encode(value, out, powers, tile, n):
    top = jnp.max(jnp.abs(value), axis=0, keepdims=True)
    power = jnp.ceil(jnp.log2(jnp.maximum(top, 1e-30)))
    code = jnp.round(value * (jnp.exp2(-power) * TOP))
    out[pl.ds(n * tile, tile), :] = code.astype(jnp.int32).astype(jnp.int16)
    powers[pl.ds(n, 1), :] = power


def flush_powers(out, powers, first):
    rows = out.shape[0] - first
    out[pl.ds(first, rows), :] = powers[pl.ds(0, rows), :].astype(jnp.int32).astype(jnp.int16)


def partial_kernel(dims, counts, *refs):
    members, tokens, cols, slots, tile = dims
    tiles, width = cols * slots, cols * tile
    parts, refs = refs[:members], refs[members:]
    messages = max(len(counts), 1)
    outs, (picks, held, total, *powers) = refs[:messages], refs[messages:]
    for p, part in enumerate(parts):
        rows = pl.ds(p * tokens, tokens)
        held[rows, :] = part[:, pl.ds(0, width)]
        picks[rows, :] = part[:, pl.ds(width, slots * tile)]
    total[...] = lax.dot_general(held[...], picks[...], (((0,), (0,)), ((), ())), preferred_element_type=jnp.float32)
    if counts:
        n = 0
        for out, count in zip(outs, counts):
            for i in range(count):
                c, k = divmod(n, slots)
                encode(total[pl.ds(c * tile, tile), pl.ds(k * tile, tile)], out, powers[0], tile, i)
                n += 1
            flush_powers(out, powers[0], count * tile)
    else:
        for n in range(tiles):
            c, k = divmod(n, slots)
            outs[0][pl.ds(n * tile, tile), :] = total[pl.ds(c * tile, tile), pl.ds(k * tile, tile)]


def join_kernel(tile, tiles, first, base_tiles, base, added, out, powers):
    for n in range(tiles):
        encode(decode(base, base_tiles, tile, first + n) + decode(added, tiles, tile, n), out, powers, tile, n)
    flush_powers(out, powers, tiles * tile)


def finish_kernel(dims, split, me_ref, mask_ref, own, out_a, out_b, inward, mid_a, mid_b, out, made, sems):
    members, _, cols, slots, tile = dims
    tiles = cols * slots

    def run(first, second, wholes):
        writes = []
        for c in range(cols):
            for k in range(slots):
                n = c * slots + k
                value = own[pl.ds(n * tile, tile), :] + (
                    decode(first, split, tile, n) if n < split else decode(second, tiles - split, tile, n - split)
                )
                for source in wholes:
                    value = value + decode(source, tiles, tile, n)
                made[c, k] = value * mask_ref[k, c].astype(jnp.float32)
            write = pltpu.make_async_copy(made.at[c], out.at[c], sems.at[c])
            write.start()
            writes.append(write)
        wait_all(writes)

    outer = (me_ref[0] < members) | (me_ref[0] >= 3 * members)
    pl.when(outer)(lambda: run(out_a, out_b, ()))
    pl.when(jnp.logical_not(outer))(lambda: run(mid_a, mid_b, (inward,)))


def grad_kernel(dims, chunks, me_ref, share_ref, rows_ref, *refs):
    members, _, cols, slots, tile = dims
    width, near = cols * tile, members // 2
    quarter = width // 4
    refs = list(refs)
    grads = [refs.pop(0) for _ in range(near)]
    inputs = [([refs.pop(0) for _ in range(members)], refs.pop(0), refs.pop(0)) for _ in chunks]
    olds, news, (weights, picks) = refs[:members], refs[members:members + near], refs[members + near:]

    def product(rows, n):
        made = lax.dot_general(rows, weights[n], (((1,), (1,)), ((), ())), preferred_element_type=jnp.float32)
        return made.astype(jnp.bfloat16)

    for n, j in enumerate(chunks):
        parts, mine, other = inputs[n]
        for i in range(3):
            rows = pl.ds(i * quarter, quarter)
            weights[i, pl.ds(pl.multiple_of(share_ref[0] * quarter, 16), quarter), :] = mine[rows, :]
            weights[i, pl.ds(pl.multiple_of((1 - share_ref[0]) * quarter, 16), quarter), :] = other[rows, :]
        picked = pl.ds(width, slots * tile)
        for p in range(members):
            olds[p][:, pl.ds(n * 2 * quarter, 2 * quarter)] = product(parts[p][:, picked], 0)
        across = owner(j, near, members, me_ref)
        for q in range(near):
            for k in range(slots):
                picks[:, pl.ds(k * tile, tile)] = grads[q][:, block(rows_ref[k, across], tile)]
            news[q][:, pl.ds(n * width, 2 * quarter)] = product(parts[q][:, picked], 1)
            news[q][:, pl.ds(n * width + 2 * quarter, 2 * quarter)] = product(picks[...], 2)


def unpack_kernel(dims, chunks, aliased, me_ref, *refs):
    members, _, cols, _, tile = dims
    width, near = cols * tile, members // 2
    half = width // 2
    count = members + near
    olds, news, out, sems = refs[:members], refs[members:count], refs[count + aliased], refs[-1]
    copies = []
    for n, j in enumerate(chunks):
        for p in range(members):
            who = owner(j, p, members, me_ref)
            copies.append((olds[p].at[:, pl.ds(n * half, half)], out.at[:, pl.ds(pl.multiple_of(who * width, 128), half)]))
            piece = news[p % near].at[:, pl.ds(n * width + (p // near) * half, half)]
            copies.append((piece, out.at[:, pl.ds(pl.multiple_of(who * width + half, 128), half)]))
    wait_all(start_all(copies, sems))


def on_device(out_grad, hidden, down_tiles, row_blocks, tile_mask):
    devices = lax.axis_size("seqt")
    members = devices // PLANES
    tokens = out_grad.shape[0]
    cols, slots, tile = down_tiles.shape[:3]
    width, tiles = cols * tile, cols * slots
    dims = (members, tokens, cols, slots, tile)
    scale_rows = -(-tiles // 16) * 16
    me = jnp.full((1,), lax.axis_index("seqt"), jnp.int32)
    row_blocks, tile_mask = row_blocks.T, tile_mask.T
    rows_early, mask_early = [pltpu.with_memory_space_constraint(value, pltpu.HBM) for value in (row_blocks, tile_mask)]
    share = jnp.full((1,), lax.axis_index("groups") & 1, jnp.int32)
    near = members // 2
    own_grad = pltpu.with_memory_space_constraint(out_grad, pltpu.VMEM)
    out_grad, hidden = [pltpu.with_memory_space_constraint(value, pltpu.HBM) for value in (out_grad, hidden)]
    bf16, f32 = jnp.bfloat16, jnp.float32
    half = members // 2
    partners = sorted(range(1, members), key=lambda p: (p < half, p))

    def call(kernel, operands, specs, outs, out_specs, scratch, **extra):
        return pl.pallas_call(
            kernel, out_shape=outs, in_specs=specs, out_specs=out_specs, scratch_shapes=scratch,
            compiler_params=pltpu.CompilerParams(vmem_limit_bytes=LIMIT), **extra,
        )(*operands)

    def permute(value, pairs):
        return pltpu.with_memory_space_constraint(lax.ppermute(value, "seqt", pairs), pltpu.VMEM)

    def inside(value, p):
        return permute(value, [(i, i ^ p) for i in range(devices)])

    def over_x(value):
        moved = lax.ppermute(value, "groups", [(i, i ^ 1) for i in range(lax.axis_size("groups"))])
        return pltpu.with_memory_space_constraint(moved, pltpu.VMEM)

    def across(value, pairs):
        return permute(value, [(a * members + i, b * members + i) for a, b in pairs for i in range(members)])

    parts = [None] * PLANES
    for chunks in ((0,), (1, 2, 3)):
        count = len(chunks) * members
        packed = call(
            functools.partial(pack_kernel, dims, chunks),
            (me, rows_early, out_grad, hidden), [SMEM, SMEM, HBM, HBM],
            [pltpu.VMEM((tokens, width + slots * tile), bf16)] * count,
            [VMEM] * count, [DMA((count * (slots + 1),))],
        )
        for n, j in enumerate(chunks):
            mine = packed[n * members:(n + 1) * members]
            arrived = {p: inside(mine[p], p) for p in partners}
            parts[j] = [mine[0]] + [arrived[p] for p in range(1, members)]

    grads = [own_grad] + [inside(out_grad, q) for q in range(1, near)]

    depth, quarter = slots * tile, width // 4
    rows = min(quarter, tile)
    crossing = call(
        functools.partial(cross_kernel, cols, slots, tile),
        (share, mask_early, pltpu.with_memory_space_constraint(down_tiles, pltpu.HBM)), [SMEM, SMEM, HBM],
        pltpu.VMEM((quarter, depth), bf16), VMEM,
        [pltpu.VMEM((quarter // rows, slots, rows, tile), bf16), DMA((quarter // rows,))],
    )
    own_rows = call(
        functools.partial(mask_kernel, cols, slots, tile), (share, mask_early, down_tiles, crossing),
        [SMEM, SMEM, VMEM, VMEM], pltpu.VMEM((2 * quarter, depth), bf16), VMEM,
        [pltpu.VMEM((2 * quarter, depth), bf16)],
    )
    bundle = call(
        bundle_kernel, (own_rows, inside(crossing, near)), [VMEM, VMEM],
        pltpu.VMEM((3 * quarter, depth), bf16), VMEM, [],
    )
    pairs, inward, middle, outward = [(0, 1), (1, 0), (2, 3), (3, 2)], [(0, 1), (3, 2)], [(1, 2), (2, 1)], [(1, 0), (2, 3)]
    e1, m1 = across(bundle, pairs), across(bundle, middle)
    m2, o1 = across(e1, middle), across(m1, outward)
    o2 = across(m2, outward)

    def pick(at_end, inner):
        return call(
            functools.partial(pick_kernel, members), (me, at_end, inner), [SMEM, VMEM, VMEM],
            pltpu.VMEM((3 * quarter, depth), bf16), VMEM, [],
        )

    shares = {3: bundle, 2: pick(e1, m1), 1: pick(o1, m2), 0: pick(o2, e1)}
    others = {j: over_x(value) for j, value in shares.items()}

    def coded(count):
        return pltpu.VMEM((count * tile + -(-count // 16) * 16, tile), jnp.int16)

    powers = pltpu.VMEM((scale_rows, tile), f32)

    def partial(j, counts):
        outs = [coded(count) for count in counts] or [pltpu.VMEM((tiles * tile, tile), f32)]
        return call(
            functools.partial(partial_kernel, dims, counts), parts[j], [VMEM] * members,
            outs, [VMEM] * len(outs),
            [
                pltpu.VMEM((members * tokens, slots * tile), bf16),
                pltpu.VMEM((members * tokens, width), bf16),
                pltpu.VMEM((width, slots * tile), f32),
            ] + ([powers] if counts else []),
        )

    def give_back(chunks):
        count = len(chunks)
        operands = [me, share, row_blocks, *grads]
        for j in chunks:
            operands += [*parts[j], shares[j], others[j]]
        products = call(
            functools.partial(grad_kernel, dims, chunks),
            operands, [SMEM] * 3 + [VMEM] * (len(operands) - 3),
            [pltpu.VMEM((tokens, count * 2 * quarter), bf16)] * members + [pltpu.VMEM((tokens, count * width), bf16)] * near,
            [VMEM] * (members + near),
            [pltpu.VMEM((3, 2 * quarter, depth), bf16), pltpu.VMEM((tokens, depth), bf16)],
        )
        arrived = {p: inside(products[p], p) for p in partners}
        olds = [products[0]] + [arrived[p] for p in range(1, members)]
        news = [products[members]] + [inside(products[members + q], q) for q in range(1, near)]
        return olds + news

    def join(count, base, base_tiles, first, added):
        return call(
            functools.partial(join_kernel, tile, count, first, base_tiles), (base, added), [VMEM, VMEM],
            coded(count), VMEM, [powers],
        )

    counts = (tiles * 5 // 8, tiles - tiles * 5 // 8)
    firsts = (0, counts[0])
    sums_0, sums_1, (sums_2,), (own,) = partial(0, counts), partial(1, counts), partial(2, (tiles,)), partial(3, ())
    i1 = [across(sums_0[n], inward) for n in range(2)]
    i2 = [across(sums_1[n], inward) for n in range(2)]
    i3 = across(sums_2, inward)
    x1, x2, last = [], [], []
    for n, (count, first) in enumerate(zip(counts, firsts)):
        x1.append(across(join(count, sums_1[n], count, 0, i1[n]), middle))
        x2.append(across(join(count, sums_2, tiles, first, i2[n]), middle))
        last.append(across(join(count, sums_0[n], count, 0, x1[n]), outward))

    sets = {"a": (2,), "b": (1, 3), "c": (0,)}
    back = {name: give_back(chunks) for name, chunks in sets.items()}

    grad_tiles = call(
        functools.partial(finish_kernel, dims, counts[0]), (me, tile_mask, own, *last, i3, *x2),
        [SMEM, SMEM] + [VMEM] * 6, jax.ShapeDtypeStruct((cols, slots, tile, tile), f32), HBM,
        [pltpu.VMEM((cols, slots, tile, tile), f32), DMA((cols,))],
    )

    def unpack(chunks, pieces, extra):
        return call(
            functools.partial(unpack_kernel, dims, chunks, len(extra)),
            (me, *pieces, *extra), [SMEM] + [VMEM] * len(pieces) + [HBM] * len(extra),
            jax.ShapeDtypeStruct(hidden.shape, bf16), HBM, [DMA((2 * members * len(chunks),))],
            input_output_aliases={1 + len(pieces): 0} if extra else {},
        )

    result = []
    for name, chunks in sets.items():
        result = [unpack(chunks, back[name], result)]
    return result[0], grad_tiles


def solution(mesh):
    return jax.shard_map(
        on_device,
        mesh=mesh,
        in_specs=(
            P(("groups", "seqt"), None),
            P(("groups", "seqt"), None),
            P("seqt", None, None, None),
            P(),
            P("seqt", None),
        ),
        out_specs=(P(("groups", "seqt"), None), P(("groups", "seqt"), None, None, None)),
        check_vma=False,
    )
```

```python
import functools

import jax
import jax.numpy as jnp
from jax import lax
from jax.experimental import pallas as pl
from jax.experimental.pallas import tpu as pltpu
from jax.sharding import PartitionSpec as P


PLANES = 4
TOP = 32000.0
LIMIT = 8 * 1024 * 1024
HBM = pl.BlockSpec(memory_space=pltpu.HBM)
SMEM = pl.BlockSpec(memory_space=pltpu.SMEM)
VMEM = pl.BlockSpec(memory_space=pltpu.VMEM)
DMA = pltpu.SemaphoreType.DMA


def start_all(copies, sems):
    started = []
    for n, (src, dst) in enumerate(copies):
        copy = pltpu.make_async_copy(src, dst, sems.at[n])
        copy.start()
        started.append(copy)
    return started


def wait_all(started):
    for copy in started:
        copy.wait()


def plane_of(j, z):
    even = z % 2 == 0
    if j == 0:
        return jnp.where(even, 3, 0)
    if j == 1:
        return jnp.where(z < 2, z + 2, z - 2)
    if j == 2:
        return jnp.where(even, 1, 2)
    return z


def owner(j, p, members, me_ref):
    z, m = me_ref[0] // members, me_ref[0] % members
    return plane_of(j, z) * members + (m ^ p)


def block(index, size):
    return pl.ds(pl.multiple_of(index * size, 128), size)


def pack_kernel(dims, chunks, me_ref, rows_ref, grad_ref, hidden_ref, *refs):
    members, _, cols, slots, tile = dims
    outs, sems = refs[:-1], refs[-1]
    width = cols * tile
    copies = []
    for n, j in enumerate(chunks):
        for p in range(members):
            out, who = outs[n * members + p], owner(j, p, members, me_ref)
            copies.append((hidden_ref.at[:, block(who, width)], out.at[:, pl.ds(0, width)]))
            for k in range(slots):
                copies.append((grad_ref.at[:, block(rows_ref[k, who], tile)], out.at[:, pl.ds(width + k * tile, tile)]))
    wait_all(start_all(copies, sems))


def cross_kernel(cols, slots, tile, share_ref, mask_ref, tiles_ref, crossing, loaded, sems):
    quarter = cols * tile // 4
    rows = min(quarter, tile)
    start = (2 + share_ref[0]) * quarter
    inner = pl.multiple_of(start % tile, 16)
    columns = [start // tile + n for n in range(quarter // rows)]
    wait_all(start_all([(tiles_ref.at[c, :, pl.ds(inner, rows), :], loaded.at[n]) for n, c in enumerate(columns)], sems))
    for n, c in enumerate(columns):
        for k in range(slots):
            factor = mask_ref[k, c].astype(jnp.float32).astype(jnp.bfloat16)
            crossing[pl.ds(n * rows, rows), pl.ds(k * tile, tile)] = loaded[n, k] * factor


def mask_kernel(cols, slots, tile, share_ref, mask_ref, tiles_ref, crossing, own, matrix):
    for c in range(cols // 2):
        for k in range(slots):
            factor = mask_ref[k, c].astype(jnp.float32).astype(jnp.bfloat16)
            matrix[pl.ds(c * tile, tile), pl.ds(k * tile, tile)] = tiles_ref[c, k] * factor
    quarter = cols * tile // 4
    own[pl.ds(0, quarter), :] = matrix[pl.ds(pl.multiple_of(share_ref[0] * quarter, 16), quarter), :]
    own[pl.ds(quarter, quarter), :] = crossing[...]


def bundle_kernel(own, crossed, out):
    rows = own.shape[0]
    out[pl.ds(0, rows), :] = own[...]
    out[pl.ds(rows, crossed.shape[0]), :] = crossed[...]


def pick_kernel(members, me_ref, at_end, inside, out):
    outer = (me_ref[0] < members) | (me_ref[0] >= 3 * members)

    @pl.when(outer)
    def _():
        out[...] = at_end[...]

    @pl.when(jnp.logical_not(outer))
    def _():
        out[...] = inside[...]


def decode(ref, tiles, tile, n):
    scale = jnp.exp2(ref[pl.ds(tiles * tile + n, 1), :].astype(jnp.float32)) * (1.0 / TOP)
    return ref[pl.ds(n * tile, tile), :].astype(jnp.float32) * scale


def encode(value, out, powers, tile, n):
    top = jnp.max(jnp.abs(value), axis=0, keepdims=True)
    power = jnp.ceil(jnp.log2(jnp.maximum(top, 1e-30)))
    code = jnp.round(value * (jnp.exp2(-power) * TOP))
    out[pl.ds(n * tile, tile), :] = code.astype(jnp.int32).astype(jnp.int16)
    powers[pl.ds(n, 1), :] = power


def flush_powers(out, powers, first):
    rows = out.shape[0] - first
    out[pl.ds(first, rows), :] = powers[pl.ds(0, rows), :].astype(jnp.int32).astype(jnp.int16)


def partial_kernel(dims, counts, *refs):
    members, tokens, cols, slots, tile = dims
    tiles, width = cols * slots, cols * tile
    parts, refs = refs[:members], refs[members:]
    messages = max(len(counts), 1)
    outs, (picks, held, total, *powers) = refs[:messages], refs[messages:]
    for p, part in enumerate(parts):
        rows = pl.ds(p * tokens, tokens)
        held[rows, :] = part[:, pl.ds(0, width)]
        picks[rows, :] = part[:, pl.ds(width, slots * tile)]
    total[...] = lax.dot_general(held[...], picks[...], (((0,), (0,)), ((), ())), preferred_element_type=jnp.float32)
    if counts:
        n = 0
        for out, count in zip(outs, counts):
            for i in range(count):
                c, k = divmod(n, slots)
                encode(total[pl.ds(c * tile, tile), pl.ds(k * tile, tile)], out, powers[0], tile, i)
                n += 1
            flush_powers(out, powers[0], count * tile)
    else:
        for n in range(tiles):
            c, k = divmod(n, slots)
            outs[0][pl.ds(n * tile, tile), :] = total[pl.ds(c * tile, tile), pl.ds(k * tile, tile)]


def join_kernel(tile, tiles, first, base_tiles, base, added, out, powers):
    for n in range(tiles):
        encode(decode(base, base_tiles, tile, first + n) + decode(added, tiles, tile, n), out, powers, tile, n)
    flush_powers(out, powers, tiles * tile)


def finish_kernel(dims, split, me_ref, mask_ref, own, out_a, out_b, inward, mid_a, mid_b, out, made, sems):
    members, _, cols, slots, tile = dims
    tiles = cols * slots

    def run(first, second, wholes):
        writes = []
        for c in range(cols):
            for k in range(slots):
                n = c * slots + k
                value = own[pl.ds(n * tile, tile), :] + (
                    decode(first, split, tile, n) if n < split else decode(second, tiles - split, tile, n - split)
                )
                for source in wholes:
                    value = value + decode(source, tiles, tile, n)
                made[c, k] = value * mask_ref[k, c].astype(jnp.float32)
            write = pltpu.make_async_copy(made.at[c], out.at[c], sems.at[c])
            write.start()
            writes.append(write)
        wait_all(writes)

    outer = (me_ref[0] < members) | (me_ref[0] >= 3 * members)
    pl.when(outer)(lambda: run(out_a, out_b, ()))
    pl.when(jnp.logical_not(outer))(lambda: run(mid_a, mid_b, (inward,)))


def grad_kernel(dims, chunks, make_old, make_new, me_ref, share_ref, rows_ref, *refs):
    members, _, cols, slots, tile = dims
    width, near = cols * tile, members // 2
    quarter = width // 4
    refs = list(refs)
    grads = [refs.pop(0) for _ in range(near)]
    inputs = [([refs.pop(0) for _ in range(members)], refs.pop(0), refs.pop(0)) for _ in chunks]
    olds = refs[:members * make_old]
    news, (weights, picks) = refs[len(olds):-2], refs[-2:]

    def product(rows, n):
        made = lax.dot_general(rows, weights[n], (((1,), (1,)), ((), ())), preferred_element_type=jnp.float32)
        return made.astype(jnp.bfloat16)

    for n, j in enumerate(chunks):
        parts, mine, other = inputs[n]
        for i in range(3):
            rows = pl.ds(i * quarter, quarter)
            weights[i, pl.ds(pl.multiple_of(share_ref[0] * quarter, 16), quarter), :] = mine[rows, :]
            weights[i, pl.ds(pl.multiple_of((1 - share_ref[0]) * quarter, 16), quarter), :] = other[rows, :]
        picked = pl.ds(width, slots * tile)
        for p in range(members * make_old):
            olds[p][:, pl.ds(n * 2 * quarter, 2 * quarter)] = product(parts[p][:, picked], 0)
        across = owner(j, near, members, me_ref)
        for q in range(near * make_new):
            for k in range(slots):
                picks[:, pl.ds(k * tile, tile)] = grads[q][:, block(rows_ref[k, across], tile)]
            news[q][:, pl.ds(n * width, 2 * quarter)] = product(parts[q][:, picked], 1)
            news[q][:, pl.ds(n * width + 2 * quarter, 2 * quarter)] = product(picks[...], 2)


def start_unpack(dims, chunks, me_ref, refs, out, sems):
    members, _, cols, _, tile = dims
    width, near = cols * tile, members // 2
    half = width // 2
    count = members + near
    olds, news = refs[:members], refs[members:count]
    copies = []
    for n, j in enumerate(chunks):
        for p in range(members):
            who = owner(j, p, members, me_ref)
            copies.append((olds[p].at[:, pl.ds(n * half, half)], out.at[:, pl.ds(pl.multiple_of(who * width, 128), half)]))
            piece = news[p % near].at[:, pl.ds(n * width + (p // near) * half, half)]
            copies.append((piece, out.at[:, pl.ds(pl.multiple_of(who * width + half, 128), half)]))
    return start_all(copies, sems)


def unpack_kernel(dims, chunks, aliased, me_ref, *refs):
    count = dims[0] + dims[0] // 2
    wait_all(start_unpack(dims, chunks, me_ref, refs[:count], refs[count + aliased], refs[-1]))


def final_kernel(dims, split, chunks, *refs):
    count = dims[0] + dims[0] // 2
    inputs, pieces, (result, tiles_out, made, tile_sems, sems) = refs[:8], refs[8:8 + count], refs[9 + count:]
    started = start_unpack(dims, chunks, refs[0], pieces, result, sems)
    finish_kernel(dims, split, *inputs, tiles_out, made, tile_sems)
    wait_all(started)


def on_device(out_grad, hidden, down_tiles, row_blocks, tile_mask):
    devices = lax.axis_size("seqt")
    members = devices // PLANES
    tokens = out_grad.shape[0]
    cols, slots, tile = down_tiles.shape[:3]
    width, tiles = cols * tile, cols * slots
    dims = (members, tokens, cols, slots, tile)
    scale_rows = -(-tiles // 16) * 16
    me = jnp.full((1,), lax.axis_index("seqt"), jnp.int32)
    row_blocks, tile_mask = row_blocks.T, tile_mask.T
    rows_early, mask_early = [pltpu.with_memory_space_constraint(value, pltpu.HBM) for value in (row_blocks, tile_mask)]
    share = jnp.full((1,), lax.axis_index("groups") & 1, jnp.int32)
    near = members // 2
    own_grad = pltpu.with_memory_space_constraint(out_grad, pltpu.VMEM)
    out_grad, hidden = [pltpu.with_memory_space_constraint(value, pltpu.HBM) for value in (out_grad, hidden)]
    bf16, f32 = jnp.bfloat16, jnp.float32
    half = members // 2
    partners = sorted(range(1, members), key=lambda p: (p < half, p))

    def call(kernel, operands, specs, outs, out_specs, scratch, **extra):
        return pl.pallas_call(
            kernel, out_shape=outs, in_specs=specs, out_specs=out_specs, scratch_shapes=scratch,
            compiler_params=pltpu.CompilerParams(vmem_limit_bytes=LIMIT), **extra,
        )(*operands)

    def permute(value, pairs):
        return pltpu.with_memory_space_constraint(lax.ppermute(value, "seqt", pairs), pltpu.VMEM)

    def inside(value, p):
        return permute(value, [(i, i ^ p) for i in range(devices)])

    def over_x(value):
        moved = lax.ppermute(value, "groups", [(i, i ^ 1) for i in range(lax.axis_size("groups"))])
        return pltpu.with_memory_space_constraint(moved, pltpu.VMEM)

    def across(value, pairs):
        return permute(value, [(a * members + i, b * members + i) for a, b in pairs for i in range(members)])

    parts = [None] * PLANES
    for chunks in ((0,), (1, 2, 3)):
        count = len(chunks) * members
        packed = call(
            functools.partial(pack_kernel, dims, chunks),
            (me, rows_early, out_grad, hidden), [SMEM, SMEM, HBM, HBM],
            [pltpu.VMEM((tokens, width + slots * tile), bf16)] * count,
            [VMEM] * count, [DMA((count * (slots + 1),))],
        )
        for n, j in enumerate(chunks):
            mine = packed[n * members:(n + 1) * members]
            arrived = {p: inside(mine[p], p) for p in partners}
            parts[j] = [mine[0]] + [arrived[p] for p in range(1, members)]

    grads = [own_grad] + [inside(out_grad, q) for q in range(1, near)]

    depth, quarter = slots * tile, width // 4
    rows = min(quarter, tile)
    crossing = call(
        functools.partial(cross_kernel, cols, slots, tile),
        (share, mask_early, pltpu.with_memory_space_constraint(down_tiles, pltpu.HBM)), [SMEM, SMEM, HBM],
        pltpu.VMEM((quarter, depth), bf16), VMEM,
        [pltpu.VMEM((quarter // rows, slots, rows, tile), bf16), DMA((quarter // rows,))],
    )
    own_rows = call(
        functools.partial(mask_kernel, cols, slots, tile), (share, mask_early, down_tiles, crossing),
        [SMEM, SMEM, VMEM, VMEM], pltpu.VMEM((2 * quarter, depth), bf16), VMEM,
        [pltpu.VMEM((2 * quarter, depth), bf16)],
    )
    bundle = call(
        bundle_kernel, (own_rows, inside(crossing, near)), [VMEM, VMEM],
        pltpu.VMEM((3 * quarter, depth), bf16), VMEM, [],
    )
    pairs, inward, middle, outward = [(0, 1), (1, 0), (2, 3), (3, 2)], [(0, 1), (3, 2)], [(1, 2), (2, 1)], [(1, 0), (2, 3)]
    e1, m1 = across(bundle, pairs), across(bundle, middle)
    m2, o1 = across(e1, middle), across(m1, outward)
    o2 = across(m2, outward)

    def pick(at_end, inner):
        return call(
            functools.partial(pick_kernel, members), (me, at_end, inner), [SMEM, VMEM, VMEM],
            pltpu.VMEM((3 * quarter, depth), bf16), VMEM, [],
        )

    shares = {3: bundle, 2: pick(e1, m1), 1: pick(o1, m2), 0: pick(o2, e1)}
    others = {j: over_x(value) for j, value in shares.items()}

    def coded(count):
        return pltpu.VMEM((count * tile + -(-count // 16) * 16, tile), jnp.int16)

    powers = pltpu.VMEM((scale_rows, tile), f32)

    def partial(j, counts):
        outs = [coded(count) for count in counts] or [pltpu.VMEM((tiles * tile, tile), f32)]
        return call(
            functools.partial(partial_kernel, dims, counts), parts[j], [VMEM] * members,
            outs, [VMEM] * len(outs),
            [
                pltpu.VMEM((members * tokens, slots * tile), bf16),
                pltpu.VMEM((members * tokens, width), bf16),
                pltpu.VMEM((width, slots * tile), f32),
            ] + ([powers] if counts else []),
        )

    def give_back(name, chunks):
        count = len(chunks)
        operands = [me, share, row_blocks, *grads]
        for j in chunks:
            operands += [*parts[j], shares[j], others[j]]
        old_shapes = [pltpu.VMEM((tokens, count * 2 * quarter), bf16)] * members
        new_shapes = [pltpu.VMEM((tokens, count * width), bf16)] * near

        def make(make_old, make_new):
            shapes = old_shapes * make_old + new_shapes * make_new
            return call(
                functools.partial(grad_kernel, dims, chunks, make_old, make_new),
                operands, [SMEM] * 3 + [VMEM] * (len(operands) - 3), shapes, [VMEM] * len(shapes),
                [pltpu.VMEM((3, 2 * quarter, depth), bf16), pltpu.VMEM((tokens, depth), bf16)],
            )

        if name == "c":
            products = [*make(True, False), *make(False, True)]
        else:
            products = make(True, True)
        arrived = {p: inside(products[p], p) for p in partners}
        olds = [products[0]] + [arrived[p] for p in range(1, members)]
        news = [products[members]] + [inside(products[members + q], q) for q in range(1, near)]
        return olds + news

    def join(count, base, base_tiles, first, added):
        return call(
            functools.partial(join_kernel, tile, count, first, base_tiles), (base, added), [VMEM, VMEM],
            coded(count), VMEM, [powers],
        )

    counts = (tiles * 5 // 8, tiles - tiles * 5 // 8)
    firsts = (0, counts[0])
    sums_0, sums_1, (sums_2,), (own,) = partial(0, counts), partial(1, counts), partial(2, (tiles,)), partial(3, ())
    i1 = [across(sums_0[n], inward) for n in range(2)]
    i2 = [across(sums_1[n], inward) for n in range(2)]
    i3 = across(sums_2, inward)
    x1, x2, last = [], [], []
    for n, (count, first) in enumerate(zip(counts, firsts)):
        x1.append(across(join(count, sums_1[n], count, 0, i1[n]), middle))
        x2.append(across(join(count, sums_2, tiles, first, i2[n]), middle))
        last.append(across(join(count, sums_0[n], count, 0, x1[n]), outward))

    sets = {"a": (2,), "b": (1, 3), "c": (0,)}
    back = {name: give_back(name, chunks) for name, chunks in sets.items()}

    def unpack(chunks, pieces, extra):
        return call(
            functools.partial(unpack_kernel, dims, chunks, len(extra)),
            (me, *pieces, *extra), [SMEM] + [VMEM] * len(pieces) + [HBM] * len(extra),
            jax.ShapeDtypeStruct(hidden.shape, bf16), HBM, [DMA((2 * members * len(chunks),))],
            input_output_aliases={1 + len(pieces): 0} if extra else {},
        )

    result = unpack(sets["b"], back["b"], [unpack(sets["a"], back["a"], [])])
    pieces = back["c"]
    return call(
        functools.partial(final_kernel, dims, counts[0], sets["c"]),
        (me, tile_mask, own, *last, i3, *x2, *pieces, result), [SMEM, SMEM] + [VMEM] * (6 + len(pieces)) + [HBM],
        [jax.ShapeDtypeStruct(hidden.shape, bf16), jax.ShapeDtypeStruct((cols, slots, tile, tile), f32)], [HBM, HBM],
        [pltpu.VMEM((cols, slots, tile, tile), f32), DMA((cols,)), DMA((2 * members,))],
        input_output_aliases={8 + len(pieces): 0},
    )


def solution(mesh):
    return jax.shard_map(
        on_device,
        mesh=mesh,
        in_specs=(
            P(("groups", "seqt"), None),
            P(("groups", "seqt"), None),
            P("seqt", None, None, None),
            P(),
            P("seqt", None),
        ),
        out_specs=(P(("groups", "seqt"), None), P(("groups", "seqt"), None, None, None)),
        check_vma=False,
    )
```

```python
import functools

import jax
import jax.numpy as jnp
from jax import lax
from jax.experimental import pallas as pl
from jax.experimental.pallas import tpu as pltpu
from jax.sharding import PartitionSpec as P


PLANES = 4
TOP = 32000.0
LIMIT = 8 * 1024 * 1024
HBM = pl.BlockSpec(memory_space=pltpu.HBM)
SMEM = pl.BlockSpec(memory_space=pltpu.SMEM)
VMEM = pl.BlockSpec(memory_space=pltpu.VMEM)
DMA = pltpu.SemaphoreType.DMA


def start_all(copies, sems):
    started = []
    for n, (src, dst) in enumerate(copies):
        copy = pltpu.make_async_copy(src, dst, sems.at[n])
        copy.start()
        started.append(copy)
    return started


def wait_all(started):
    for copy in started:
        copy.wait()


def plane_of(j, z):
    even = z % 2 == 0
    if j == 0:
        return jnp.where(even, 3, 0)
    if j == 1:
        return jnp.where(z < 2, z + 2, z - 2)
    if j == 2:
        return jnp.where(even, 1, 2)
    return z


def owner(j, p, members, me_ref):
    z, m = me_ref[0] // members, me_ref[0] % members
    return plane_of(j, z) * members + (m ^ p)


def block(index, size):
    return pl.ds(pl.multiple_of(index * size, 128), size)


def pack_kernel(dims, chunks, me_ref, rows_ref, grad_ref, hidden_ref, *refs):
    members, _, cols, slots, tile = dims
    outs, sems = refs[:-1], refs[-1]
    width = cols * tile
    copies = []
    for n, j in enumerate(chunks):
        for p in range(members):
            out, who = outs[n * members + p], owner(j, p, members, me_ref)
            copies.append((hidden_ref.at[:, block(who, width)], out.at[:, pl.ds(0, width)]))
            for k in range(slots):
                copies.append((grad_ref.at[:, block(rows_ref[k, who], tile)], out.at[:, pl.ds(width + k * tile, tile)]))
    wait_all(start_all(copies, sems))


def cross_kernel(cols, slots, tile, share_ref, mask_ref, tiles_ref, crossing, loaded, sems):
    quarter = cols * tile // 4
    rows = min(quarter, tile)
    start = (2 + share_ref[0]) * quarter
    inner = pl.multiple_of(start % tile, 16)
    columns = [start // tile + n for n in range(quarter // rows)]
    wait_all(start_all([(tiles_ref.at[c, :, pl.ds(inner, rows), :], loaded.at[n]) for n, c in enumerate(columns)], sems))
    for n, c in enumerate(columns):
        for k in range(slots):
            factor = mask_ref[k, c].astype(jnp.float32).astype(jnp.bfloat16)
            crossing[pl.ds(n * rows, rows), pl.ds(k * tile, tile)] = loaded[n, k] * factor


def mask_kernel(cols, slots, tile, share_ref, mask_ref, tiles_ref, crossing, own, matrix):
    for c in range(cols // 2):
        for k in range(slots):
            factor = mask_ref[k, c].astype(jnp.float32).astype(jnp.bfloat16)
            matrix[pl.ds(c * tile, tile), pl.ds(k * tile, tile)] = tiles_ref[c, k] * factor
    quarter = cols * tile // 4
    own[pl.ds(0, quarter), :] = matrix[pl.ds(pl.multiple_of(share_ref[0] * quarter, 16), quarter), :]
    own[pl.ds(quarter, quarter), :] = crossing[...]


def bundle_kernel(own, crossed, out):
    rows = own.shape[0]
    out[pl.ds(0, rows), :] = own[...]
    out[pl.ds(rows, crossed.shape[0]), :] = crossed[...]


def pick_kernel(members, me_ref, at_end, inside, out):
    outer = (me_ref[0] < members) | (me_ref[0] >= 3 * members)

    @pl.when(outer)
    def _():
        out[...] = at_end[...]

    @pl.when(jnp.logical_not(outer))
    def _():
        out[...] = inside[...]


def decode(ref, tiles, tile, n):
    scale = jnp.exp2(ref[pl.ds(tiles * tile + n, 1), :].astype(jnp.float32)) * (1.0 / TOP)
    return ref[pl.ds(n * tile, tile), :].astype(jnp.float32) * scale


def encode(value, out, powers, tile, n):
    top = jnp.max(jnp.abs(value), axis=0, keepdims=True)
    power = jnp.ceil(jnp.log2(jnp.maximum(top, 1e-30)))
    code = jnp.round(value * (jnp.exp2(-power) * TOP))
    out[pl.ds(n * tile, tile), :] = code.astype(jnp.int32).astype(jnp.int16)
    powers[pl.ds(n, 1), :] = power


def flush_powers(out, powers, first):
    rows = out.shape[0] - first
    out[pl.ds(first, rows), :] = powers[pl.ds(0, rows), :].astype(jnp.int32).astype(jnp.int16)


def partial_kernel(dims, counts, *refs):
    members, tokens, cols, slots, tile = dims
    tiles, width = cols * slots, cols * tile
    parts, refs = refs[:members], refs[members:]
    messages = max(len(counts), 1)
    outs, (picks, held, total, *powers) = refs[:messages], refs[messages:]
    for p, part in enumerate(parts):
        rows = pl.ds(p * tokens, tokens)
        held[rows, :] = part[:, pl.ds(0, width)]
        picks[rows, :] = part[:, pl.ds(width, slots * tile)]
    total[...] = lax.dot_general(held[...], picks[...], (((0,), (0,)), ((), ())), preferred_element_type=jnp.float32)
    if counts:
        n = 0
        for out, count in zip(outs, counts):
            for i in range(count):
                c, k = divmod(n, slots)
                encode(total[pl.ds(c * tile, tile), pl.ds(k * tile, tile)], out, powers[0], tile, i)
                n += 1
            flush_powers(out, powers[0], count * tile)
    else:
        for n in range(tiles):
            c, k = divmod(n, slots)
            outs[0][pl.ds(n * tile, tile), :] = total[pl.ds(c * tile, tile), pl.ds(k * tile, tile)]


def join_kernel(tile, tiles, first, base_tiles, base, added, out, powers):
    for n in range(tiles):
        encode(decode(base, base_tiles, tile, first + n) + decode(added, tiles, tile, n), out, powers, tile, n)
    flush_powers(out, powers, tiles * tile)


def finish_kernel(dims, split, me_ref, mask_ref, own, out_a, out_b, inward, mid_a, mid_b, out, made, sems):
    members, _, cols, slots, tile = dims
    tiles = cols * slots

    def run(first, second, wholes):
        writes = []
        for c in range(cols):
            for k in range(slots):
                n = c * slots + k
                value = own[pl.ds(n * tile, tile), :] + (
                    decode(first, split, tile, n) if n < split else decode(second, tiles - split, tile, n - split)
                )
                for source in wholes:
                    value = value + decode(source, tiles, tile, n)
                made[c, k] = value * mask_ref[k, c].astype(jnp.float32)
            write = pltpu.make_async_copy(made.at[c], out.at[c], sems.at[c])
            write.start()
            writes.append(write)
        wait_all(writes)

    outer = (me_ref[0] < members) | (me_ref[0] >= 3 * members)
    pl.when(outer)(lambda: run(out_a, out_b, ()))
    pl.when(jnp.logical_not(outer))(lambda: run(mid_a, mid_b, (inward,)))


def grad_kernel(dims, chunks, make_old, make_new, me_ref, share_ref, rows_ref, *refs):
    members, _, cols, slots, tile = dims
    width, near = cols * tile, members // 2
    quarter = width // 4
    refs = list(refs)
    grads = [refs.pop(0) for _ in range(near)]
    inputs = [([refs.pop(0) for _ in range(members)], refs.pop(0), refs.pop(0)) for _ in chunks]
    olds = refs[:members * make_old]
    news, (weights, picks) = refs[len(olds):-2], refs[-2:]

    def product(rows, n):
        made = lax.dot_general(rows, weights[n], (((1,), (1,)), ((), ())), preferred_element_type=jnp.float32)
        return made.astype(jnp.bfloat16)

    for n, j in enumerate(chunks):
        parts, mine, other = inputs[n]
        for i in range(3):
            rows = pl.ds(i * quarter, quarter)
            weights[i, pl.ds(pl.multiple_of(share_ref[0] * quarter, 16), quarter), :] = mine[rows, :]
            weights[i, pl.ds(pl.multiple_of((1 - share_ref[0]) * quarter, 16), quarter), :] = other[rows, :]
        picked = pl.ds(width, slots * tile)
        for p in range(members * make_old):
            olds[p][:, pl.ds(n * 2 * quarter, 2 * quarter)] = product(parts[p][:, picked], 0)
        across = owner(j, near, members, me_ref)
        for q in range(near * make_new):
            for k in range(slots):
                picks[:, pl.ds(k * tile, tile)] = grads[q][:, block(rows_ref[k, across], tile)]
            news[q][:, pl.ds(n * width, 2 * quarter)] = product(parts[q][:, picked], 1)
            news[q][:, pl.ds(n * width + 2 * quarter, 2 * quarter)] = product(picks[...], 2)


def start_unpack(dims, chunks, me_ref, refs, out, sems):
    members, _, cols, _, tile = dims
    width, near = cols * tile, members // 2
    half = width // 2
    count = members + near
    olds, news = refs[:members], refs[members:count]
    copies = []
    for n, j in enumerate(chunks):
        for p in range(members):
            who = owner(j, p, members, me_ref)
            copies.append((olds[p].at[:, pl.ds(n * half, half)], out.at[:, pl.ds(pl.multiple_of(who * width, 128), half)]))
            piece = news[p % near].at[:, pl.ds(n * width + (p // near) * half, half)]
            copies.append((piece, out.at[:, pl.ds(pl.multiple_of(who * width + half, 128), half)]))
    return start_all(copies, sems)


def unpack_kernel(dims, chunks, aliased, me_ref, *refs):
    count = dims[0] + dims[0] // 2
    wait_all(start_unpack(dims, chunks, me_ref, refs[:count], refs[count + aliased], refs[-1]))


def on_device(out_grad, hidden, down_tiles, row_blocks, tile_mask):
    devices = lax.axis_size("seqt")
    members = devices // PLANES
    tokens = out_grad.shape[0]
    cols, slots, tile = down_tiles.shape[:3]
    width, tiles = cols * tile, cols * slots
    dims = (members, tokens, cols, slots, tile)
    scale_rows = -(-tiles // 16) * 16
    me = jnp.full((1,), lax.axis_index("seqt"), jnp.int32)
    row_blocks, tile_mask = row_blocks.T, tile_mask.T
    rows_early, mask_early = [pltpu.with_memory_space_constraint(value, pltpu.HBM) for value in (row_blocks, tile_mask)]
    share = jnp.full((1,), lax.axis_index("groups") & 1, jnp.int32)
    near = members // 2
    own_grad = pltpu.with_memory_space_constraint(out_grad, pltpu.VMEM)
    out_grad, hidden = [pltpu.with_memory_space_constraint(value, pltpu.HBM) for value in (out_grad, hidden)]
    bf16, f32 = jnp.bfloat16, jnp.float32
    half = members // 2
    partners = sorted(range(1, members), key=lambda p: (p < half, p))

    def call(kernel, operands, specs, outs, out_specs, scratch, **extra):
        return pl.pallas_call(
            kernel, out_shape=outs, in_specs=specs, out_specs=out_specs, scratch_shapes=scratch,
            compiler_params=pltpu.CompilerParams(vmem_limit_bytes=LIMIT), **extra,
        )(*operands)

    def permute(value, pairs):
        return pltpu.with_memory_space_constraint(lax.ppermute(value, "seqt", pairs), pltpu.VMEM)

    def inside(value, p):
        return permute(value, [(i, i ^ p) for i in range(devices)])

    def over_x(value):
        moved = lax.ppermute(value, "groups", [(i, i ^ 1) for i in range(lax.axis_size("groups"))])
        return pltpu.with_memory_space_constraint(moved, pltpu.VMEM)

    def across(value, pairs):
        return permute(value, [(a * members + i, b * members + i) for a, b in pairs for i in range(members)])

    parts = [None] * PLANES
    for chunks in ((0,), (1, 2, 3)):
        count = len(chunks) * members
        packed = call(
            functools.partial(pack_kernel, dims, chunks),
            (me, rows_early, out_grad, hidden), [SMEM, SMEM, HBM, HBM],
            [pltpu.VMEM((tokens, width + slots * tile), bf16)] * count,
            [VMEM] * count, [DMA((count * (slots + 1),))],
        )
        for n, j in enumerate(chunks):
            mine = packed[n * members:(n + 1) * members]
            arrived = {p: inside(mine[p], p) for p in partners}
            parts[j] = [mine[0]] + [arrived[p] for p in range(1, members)]

    grads = [own_grad] + [inside(out_grad, q) for q in range(1, near)]

    depth, quarter = slots * tile, width // 4
    rows = min(quarter, tile)
    crossing = call(
        functools.partial(cross_kernel, cols, slots, tile),
        (share, mask_early, pltpu.with_memory_space_constraint(down_tiles, pltpu.HBM)), [SMEM, SMEM, HBM],
        pltpu.VMEM((quarter, depth), bf16), VMEM,
        [pltpu.VMEM((quarter // rows, slots, rows, tile), bf16), DMA((quarter // rows,))],
    )
    own_rows = call(
        functools.partial(mask_kernel, cols, slots, tile), (share, mask_early, down_tiles, crossing),
        [SMEM, SMEM, VMEM, VMEM], pltpu.VMEM((2 * quarter, depth), bf16), VMEM,
        [pltpu.VMEM((2 * quarter, depth), bf16)],
    )
    bundle = call(
        bundle_kernel, (own_rows, inside(crossing, near)), [VMEM, VMEM],
        pltpu.VMEM((3 * quarter, depth), bf16), VMEM, [],
    )
    pairs, inward, middle, outward = [(0, 1), (1, 0), (2, 3), (3, 2)], [(0, 1), (3, 2)], [(1, 2), (2, 1)], [(1, 0), (2, 3)]
    e1, m1 = across(bundle, pairs), across(bundle, middle)
    m2, o1 = across(e1, middle), across(m1, outward)
    o2 = across(m2, outward)

    def pick(at_end, inner):
        return call(
            functools.partial(pick_kernel, members), (me, at_end, inner), [SMEM, VMEM, VMEM],
            pltpu.VMEM((3 * quarter, depth), bf16), VMEM, [],
        )

    shares = {3: bundle, 2: pick(e1, m1), 1: pick(o1, m2), 0: pick(o2, e1)}
    others = {j: over_x(value) for j, value in shares.items()}

    def coded(count):
        return pltpu.VMEM((count * tile + -(-count // 16) * 16, tile), jnp.int16)

    powers = pltpu.VMEM((scale_rows, tile), f32)

    def partial(j, counts):
        outs = [coded(count) for count in counts] or [pltpu.VMEM((tiles * tile, tile), f32)]
        return call(
            functools.partial(partial_kernel, dims, counts), parts[j], [VMEM] * members,
            outs, [VMEM] * len(outs),
            [
                pltpu.VMEM((members * tokens, slots * tile), bf16),
                pltpu.VMEM((members * tokens, width), bf16),
                pltpu.VMEM((width, slots * tile), f32),
            ] + ([powers] if counts else []),
        )

    def give_back(name, chunks):
        count = len(chunks)
        operands = [me, share, row_blocks, *grads]
        for j in chunks:
            operands += [*parts[j], shares[j], others[j]]
        old_shapes = [pltpu.VMEM((tokens, count * 2 * quarter), bf16)] * members
        new_shapes = [pltpu.VMEM((tokens, count * width), bf16)] * near

        def make(make_old, make_new):
            shapes = old_shapes * make_old + new_shapes * make_new
            return call(
                functools.partial(grad_kernel, dims, chunks, make_old, make_new),
                operands, [SMEM] * 3 + [VMEM] * (len(operands) - 3), shapes, [VMEM] * len(shapes),
                [pltpu.VMEM((3, 2 * quarter, depth), bf16), pltpu.VMEM((tokens, depth), bf16)],
            )

        if name == "c":
            products = [*make(True, False), *make(False, True)]
        else:
            products = make(True, True)
        arrived = {p: inside(products[p], p) for p in partners}
        olds = [products[0]] + [arrived[p] for p in range(1, members)]
        news = [products[members]] + [inside(products[members + q], q) for q in range(1, near)]
        return olds + news

    def join(count, base, base_tiles, first, added):
        return call(
            functools.partial(join_kernel, tile, count, first, base_tiles), (base, added), [VMEM, VMEM],
            coded(count), VMEM, [powers],
        )

    counts = (tiles * 5 // 8, tiles - tiles * 5 // 8)
    firsts = (0, counts[0])
    sums_0, sums_1, (sums_2,), (own,) = partial(0, counts), partial(1, counts), partial(2, (tiles,)), partial(3, ())
    i1 = [across(sums_0[n], inward) for n in range(2)]
    i2 = [across(sums_1[n], inward) for n in range(2)]
    i3 = across(sums_2, inward)
    x1, x2, last = [], [], []
    for n, (count, first) in enumerate(zip(counts, firsts)):
        x1.append(across(join(count, sums_1[n], count, 0, i1[n]), middle))
        x2.append(across(join(count, sums_2, tiles, first, i2[n]), middle))
        last.append(across(join(count, sums_0[n], count, 0, x1[n]), outward))

    sets = {"a": (2,), "b": (1, 3), "c": (0,)}
    back = {name: give_back(name, chunks) for name, chunks in sets.items()}

    grad_tiles = call(
        functools.partial(finish_kernel, dims, counts[0]), (me, tile_mask, own, *last, i3, *x2),
        [SMEM, SMEM] + [VMEM] * 6, jax.ShapeDtypeStruct((cols, slots, tile, tile), f32), HBM,
        [pltpu.VMEM((cols, slots, tile, tile), f32), DMA((cols,))],
    )

    def unpack(chunks, pieces, extra):
        return call(
            functools.partial(unpack_kernel, dims, chunks, len(extra)),
            (me, *pieces, *extra), [SMEM] + [VMEM] * len(pieces) + [HBM] * len(extra),
            jax.ShapeDtypeStruct(hidden.shape, bf16), HBM, [DMA((2 * members * len(chunks),))],
            input_output_aliases={1 + len(pieces): 0} if extra else {},
        )

    result = []
    for name, chunks in sets.items():
        result = [unpack(chunks, back[name], result)]
    return result[0], grad_tiles


def solution(mesh):
    return jax.shard_map(
        on_device,
        mesh=mesh,
        in_specs=(
            P(("groups", "seqt"), None),
            P(("groups", "seqt"), None),
            P("seqt", None, None, None),
            P(),
            P("seqt", None),
        ),
        out_specs=(P(("groups", "seqt"), None), P(("groups", "seqt"), None, None, None)),
        check_vma=False,
    )
```
